32 devices in a mesh: seq: 4 (over z), head: 4 (over y, x), batch: 2 (over core).
Axes of the slice: x: 2, y: 2, z: 4, core: 2. Of those that a mesh axis runs over, the one named last changes fastest.
Arguments:
- hidden: bfloat16 [2048, 2880], P(('batch', 'seq')), parts along dimension 0, may hold values from -20 to 20
- dest_pos: int32 [2048], P(('batch', 'seq')), parts along dimension 0, may hold values from 0 to 1023, as said below
- chosen_len: int32 [4], P('batch'), parts along dimension 0, may hold values from 128 to 384
- token_logp: float32 [2048], P(('batch', 'seq')), parts along dimension 0, may hold values from -12 to -0.05
- head_grad: bfloat16 [2048, 4096], P(('batch', 'seq'), 'head'), parts along dimension 0, may hold values from -6 to 6
- q_weight: bfloat16 [2880, 4096], P(None, 'head'), may hold values from -1 to 1
- key_value_weight: bfloat16 [2880, 8, 128], P(None, 'head'), may hold values from -1 to 1
- sinks: float32 [64], P('head'), may hold values from 2 to 6
Outputs:
- grad_hidden: bfloat16 [2048, 2880], P(('batch', 'seq')), parts along dimension 0
- pair_loss: float32 [4], P('batch'), parts along dimension 0
The draws below stay inside these ranges and needn't reach their ends.
There are 2 independent parts, one for each index of `batch`. The reference program is written for one: setup_inputs(seed, part) draws one part's arguments, and reference() takes and returns one part's arrays. A program takes and returns all parts, laid end to end along the dimension named above; an argument that names none is the same for every part. Nothing has to cross between parts.
Inputs may be any that keep to these rules, and one draw needn't show every extreme that they name: dest_pos is a permutation of the positions of one part; balanced device b holds positions b * 256 to (b + 1) * 256 - 1; the 256 rows of one loader device send at most 65 rows to any one balanced device, and exactly 65 to some. `chosen_len`: pair p occupies the positions t with (t + 64) mod 1024 from p * 512 to (p + 1) * 512 - 1, its chosen response first in that rotated order.
All inputs are finite; a program needn't handle non-finite values.
Results may differ from the reference program's by a relative error of at most 0.023.
The reference program's roundings to bfloat16 on the way count: a program that leaves them out, or rounds other values in their place, can miss the bound.
Values may be sent and summed in bfloat16 or wider, within the bound.
A program may use at most 64 MiB of HBM per device.

```python
import jax
import jax.numpy as jnp
from jax import lax

MODEL_WIDTH = 2880
QUERY_HEADS = 64
KEY_VALUE_HEADS = 8
HEAD_SIZE = 64
WINDOW = 128
TOK_DEV = 256
PAIR_POSITIONS = 512
TOKEN_COUNT = 1024
PAIR_COUNT = 2
LEAD = 64
N_HEAD = 4


def weight_parts(key):
    start_offset = jnp.clip(jax.random.normal(jax.random.fold_in(key, 11), (MODEL_WIDTH, QUERY_HEADS * HEAD_SIZE), jnp.float32), -6.0, 6.0) * MODEL_WIDTH ** (-0.5)
    new_values = jnp.clip(jax.random.normal(jax.random.fold_in(key, 12), (MODEL_WIDTH, KEY_VALUE_HEADS, 2 * HEAD_SIZE), jnp.float32), -6.0, 6.0) * MODEL_WIDTH ** (-0.5)
    return (start_offset, new_values)


def draw_q_weight(key, part):
    start_offset, new_values = weight_parts(key)
    return start_offset.astype(jnp.bfloat16)


def draw_key_value_weight(key, part):
    start_offset, new_values = weight_parts(key)
    return new_values.astype(jnp.bfloat16)


def draw_hidden(key, part):
    values = jnp.clip(jax.random.normal(jax.random.fold_in(key, 24), (TOKEN_COUNT, MODEL_WIDTH), jnp.float32), -6.0, 6.0)
    return values.astype(jnp.bfloat16)


def label_ranks(labels, count_dev):
    device_ids = jnp.arange(count_dev, dtype=jnp.int32)
    onehot = (labels[:, :, None] == device_ids[None, None, :]).astype(jnp.int32)
    before = jnp.cumsum(onehot, axis=1) - onehot
    return jnp.sum(before * onehot, axis=2)


def draw_dest_pos(key, part):
    count_dev = TOKEN_COUNT // TOK_DEV
    row_count = TOK_DEV
    base_count = row_count // count_dev
    device_ids = jnp.arange(count_dev, dtype=jnp.int32)
    row_ids = jnp.arange(row_count, dtype=jnp.int32)
    order = jax.random.permutation(jax.random.fold_in(key, 31), count_dev).astype(jnp.int32)
    shifted = jnp.roll(order, -1)
    counts = base_count + (device_ids[None, :] == order[:, None]).astype(jnp.int32) - (device_ids[None, :] == shifted[:, None]).astype(jnp.int32)
    src_cum = jnp.cumsum(counts, axis=1)
    src_label = jnp.sum((src_cum[:, None, :] <= row_ids[None, :, None]).astype(jnp.int32), axis=2)
    dst_cum = jnp.cumsum(counts, axis=0).T
    dst_label = jnp.sum((dst_cum[:, None, :] <= row_ids[None, :, None]).astype(jnp.int32), axis=2)
    src_keys = jax.random.split(jax.random.fold_in(key, 32), count_dev)
    dst_keys = jax.random.split(jax.random.fold_in(key, 33), count_dev)
    src_perm = jax.vmap(lambda item: jax.random.permutation(item, row_count))(src_keys).astype(jnp.int32)
    dst_perm = jax.vmap(lambda item: jax.random.permutation(item, row_count))(dst_keys).astype(jnp.int32)
    src_label = jnp.take_along_axis(src_label, src_perm, axis=1)
    dst_label = jnp.take_along_axis(dst_label, dst_perm, axis=1)
    src_rank = label_ranks(src_label, count_dev)
    dst_rank = label_ranks(dst_label, count_dev)
    table = jnp.zeros((count_dev, count_dev * row_count), jnp.int32)
    table = table.at[device_ids[:, None], dst_label * row_count + dst_rank].set(jnp.broadcast_to(row_ids[None, :], (count_dev, row_count)))
    slot_pos = table[src_label, device_ids[:, None] * row_count + src_rank]
    return (src_label * row_count + slot_pos).reshape(-1).astype(jnp.int32)


def block_scale(own_key, extent, shards, smallest, high):
    gain = 1.0
    for dim, shards_of in shards:
        draws = jax.random.uniform(jax.random.fold_in(jax.random.fold_in(own_key, 6), dim), (shards_of,), jnp.float32, smallest / len(shards), high / len(shards))
        gain = gain * jnp.repeat(jnp.exp(draws), extent[dim] // shards_of).reshape((-1,) + (1,) * (len(extent) - 1 - dim))
    return gain


def normal_values(stream_key, dims, scale, bound, shards=(), kind=jnp.bfloat16):
    array = scale * jax.random.normal(stream_key, dims, jnp.float32)
    if shards:
        array = array * block_scale(stream_key, dims, shards, -0.22, 0.18)
    return jnp.clip(array, -bound, bound).astype(kind)


def setup_inputs(seed: int = 0, part: int = 0) -> dict:
    keys = jax.random.split(jax.random.key(seed), 9)
    part_splits = jax.random.split(jax.random.fold_in(keys[8], part), 9)
    hidden = draw_hidden(jax.random.fold_in(jax.random.fold_in(keys[8], part), 71), part)
    dest_pos = draw_dest_pos(jax.random.fold_in(jax.random.fold_in(keys[8], part), 71), part)
    chosen_len = jax.random.randint(part_splits[2], (PAIR_COUNT,), PAIR_POSITIONS // 4, 3 * PAIR_POSITIONS // 4 + 1).astype(jnp.int32)
    token_logp = jnp.clip(-12.0 + 11.95 * jax.random.uniform(part_splits[3], (TOKEN_COUNT,), jnp.float32) ** block_scale(part_splits[3], (TOKEN_COUNT,), ((0, 4),), -0.2, 0.2), -12.0, -0.05)
    head_grad = normal_values(part_splits[4], (TOKEN_COUNT, QUERY_HEADS * HEAD_SIZE), 1.0, 6.0, ((0, 4), (1, 4)))
    q_weight = draw_q_weight(jax.random.fold_in(keys[8], 71), part)
    key_value_weight = draw_key_value_weight(jax.random.fold_in(keys[8], 71), part)
    sinks = jnp.clip(2.0 + 4.0 * jax.random.uniform(keys[7], (QUERY_HEADS,), jnp.float32) ** block_scale(keys[7], (QUERY_HEADS,), ((0, 4),), -0.2, 0.2), 2.0, 6.0)
    return dict(hidden=hidden, dest_pos=dest_pos, chosen_len=chosen_len, token_logp=token_logp, head_grad=head_grad, q_weight=q_weight, key_value_weight=key_value_weight, sinks=sinks)


BETA = 2.0
GAMMA = 1.0
LOSS_SCALE = 256.0
NEG_FILL = -1.0e30


def pair_block(args):
    q_block, kv_block, grad_block, reject_block, pos_block, sink_logits = args
    scale = HEAD_SIZE ** -0.5
    key_part = kv_block[..., :HEAD_SIZE].astype(jnp.float32)
    value_part = kv_block[..., HEAD_SIZE:].astype(jnp.float32)
    offset = pos_block[:, None] - pos_block[None, :]
    allowed = (offset >= 0) & (offset < WINDOW) & (reject_block[:, None] == reject_block[None, :])
    scores = jnp.einsum('qkgd,skd->kgqs', q_block.astype(jnp.float32), key_part) * scale
    masked = jnp.where(allowed[None, None], scores, NEG_FILL)
    row_max = jnp.maximum(jnp.max(masked, axis=-1), sink_logits[:, :, None])
    expo = jnp.where(allowed[None, None], jnp.exp(masked - row_max[..., None]), 0.0)
    denom = jnp.exp(sink_logits[:, :, None] - row_max) + jnp.sum(expo, axis=-1)
    probs = expo / denom[..., None]
    probs_b = probs.astype(jnp.bfloat16)
    grad_f = grad_block.astype(jnp.float32)
    attn_out = jnp.einsum('kgqs,skd->kgqd', probs_b.astype(jnp.float32), value_part)
    row_dot = jnp.einsum('qkgd,kgqd->kgq', grad_f, attn_out)
    prob_grad = jnp.einsum('qkgd,skd->kgqs', grad_f, value_part)
    score_grad = (probs * (prob_grad - row_dot[..., None])).astype(jnp.bfloat16).astype(jnp.float32)
    query_grad = (jnp.einsum('kgqs,skd->qkgd', score_grad, key_part) * scale).astype(jnp.bfloat16)
    key_grad = jnp.einsum('kgqs,qkgd->skd', score_grad, q_block.astype(jnp.float32)) * scale
    value_grad = jnp.einsum('kgqs,qkgd->skd', probs_b.astype(jnp.float32), grad_f)
    key_value_gradient = jnp.concatenate([key_grad, value_grad], axis=-1).astype(jnp.bfloat16)
    return query_grad, key_value_gradient


def reference(hidden, dest_pos, chosen_len, token_logp, head_grad, q_weight, key_value_weight, sinks):
    heads_per_group = QUERY_HEADS // KEY_VALUE_HEADS
    evened_rows = jnp.zeros_like(hidden).at[dest_pos.astype(jnp.int32)].set(hidden)
    query_rows = jnp.dot(evened_rows, q_weight, preferred_element_type=jnp.float32).astype(jnp.bfloat16)
    key_value_rows = jnp.dot(evened_rows, key_value_weight.reshape(MODEL_WIDTH, KEY_VALUE_HEADS * 2 * HEAD_SIZE), preferred_element_type=jnp.float32)
    key_value_rows = key_value_rows.astype(jnp.bfloat16).reshape(TOKEN_COUNT, KEY_VALUE_HEADS, 2 * HEAD_SIZE)
    position = jnp.arange(TOKEN_COUNT, dtype=jnp.int32)
    rotated = (position + LEAD) % TOKEN_COUNT
    pair_index = rotated // PAIR_POSITIONS
    within = rotated % PAIR_POSITIONS
    rejected = (within >= chosen_len[pair_index]).astype(jnp.int32)
    segment = 2 * pair_index + rejected
    seg_totals = jax.ops.segment_sum(token_logp, segment, num_segments=2 * PAIR_COUNT).reshape(PAIR_COUNT, 2)
    chosen_f = chosen_len.astype(jnp.float32)
    reject_f = (PAIR_POSITIONS - chosen_len).astype(jnp.float32)
    margin = BETA * (seg_totals[:, 0] / chosen_f - seg_totals[:, 1] / reject_f) - GAMMA
    pair_loss = jax.nn.softplus(-margin)
    weight_pair = jax.nn.sigmoid(-margin) * BETA * LOSS_SCALE
    coef = jnp.stack([-weight_pair / chosen_f, weight_pair / reject_f], axis=1).reshape(-1)
    output_gradient = (coef[segment][:, None] * head_grad.astype(jnp.float32)).astype(jnp.bfloat16)
    sink_logits = sinks.reshape(KEY_VALUE_HEADS, heads_per_group)
    query_tiles = jnp.roll(query_rows, LEAD, axis=0).reshape(PAIR_COUNT, PAIR_POSITIONS, KEY_VALUE_HEADS, heads_per_group, HEAD_SIZE)
    key_value_tiles = jnp.roll(key_value_rows, LEAD, axis=0).reshape(PAIR_COUNT, PAIR_POSITIONS, KEY_VALUE_HEADS, 2 * HEAD_SIZE)
    gradient_tiles = jnp.roll(output_gradient, LEAD, axis=0).reshape(PAIR_COUNT, PAIR_POSITIONS, KEY_VALUE_HEADS, heads_per_group, HEAD_SIZE)
    reject_blocks = jnp.roll(rejected, LEAD, axis=0).reshape(PAIR_COUNT, PAIR_POSITIONS)
    position_blocks = jnp.roll(position, LEAD, axis=0).reshape(PAIR_COUNT, PAIR_POSITIONS)

    def one_pair(items):
        return pair_block((items[0], items[1], items[2], items[3], items[4], sink_logits))

    query_grad, key_value_gradient = lax.map(one_pair, (query_tiles, key_value_tiles, gradient_tiles, reject_blocks, position_blocks))
    query_grad = jnp.roll(query_grad.reshape(TOKEN_COUNT, QUERY_HEADS * HEAD_SIZE), -LEAD, axis=0)
    key_value_gradient = jnp.roll(key_value_gradient.reshape(TOKEN_COUNT, KEY_VALUE_HEADS * 2 * HEAD_SIZE), -LEAD, axis=0)
    query_grad = query_grad.reshape(TOKEN_COUNT, N_HEAD, QUERY_HEADS * HEAD_SIZE // N_HEAD).transpose(1, 0, 2)
    key_value_gradient = key_value_gradient.reshape(TOKEN_COUNT, N_HEAD, KEY_VALUE_HEADS * 2 * HEAD_SIZE // N_HEAD).transpose(1, 0, 2)
    q_groups = q_weight.reshape(MODEL_WIDTH, N_HEAD, QUERY_HEADS * HEAD_SIZE // N_HEAD).transpose(1, 0, 2)
    key_value_groups = key_value_weight.reshape(MODEL_WIDTH, N_HEAD, KEY_VALUE_HEADS * 2 * HEAD_SIZE // N_HEAD).transpose(1, 0, 2)

    def add_group(total, items):
        dq_part, dkv_part, wq_part, wkv_part = items
        part_sum = lax.dot_general(dq_part, wq_part, (((1,), (1,)), ((), ())), preferred_element_type=jnp.float32)
        part_sum = part_sum + lax.dot_general(dkv_part, wkv_part, (((1,), (1,)), ((), ())), preferred_element_type=jnp.float32)
        rounded = lax.optimization_barrier(part_sum.astype(jnp.bfloat16))
        return total + rounded.astype(jnp.float32), None

    total, _ = lax.scan(add_group, jnp.zeros((TOKEN_COUNT, MODEL_WIDTH), jnp.float32), (query_grad, key_value_gradient, q_groups, key_value_groups))
    return total.astype(jnp.bfloat16), pair_loss
```

```python
import functools

import jax
import jax.numpy as jnp
from jax import lax
from jax.experimental import pallas as pl
from jax.experimental.pallas import tpu as pltpu
from jax.sharding import PartitionSpec as P

WINDOW = 128
PAIR_POSITIONS = 512
BETA = 2.0
GAMMA = 1.0
LOSS_SCALE = 256.0
NEG_FILL = -1e30
LANES = 128
CHUNK = 256
OUT_CHUNKS = 10
F32 = jnp.float32
BF16 = jnp.bfloat16
MESH = pl.DeviceIdType.MESH


def dot_nn(a, b):
    return lax.dot_general(a, b, (((1,), (0,)), ((), ())), preferred_element_type=F32)


def dot_nt(a, b):
    return lax.dot_general(a, b, (((1,), (1,)), ((), ())), preferred_element_type=F32)


def dot_tn(a, b):
    return lax.dot_general(a, b, (((0,), (0,)), ((), ())), preferred_element_type=F32)


def iota(shape, dim):
    return lax.broadcasted_iota(jnp.int32, shape, dim)


def log2(n):
    assert n & (n - 1) == 0
    return n.bit_length() - 1


def chunk_bounds(feat, n):
    unit = 16 * n
    units = -(-feat // unit)
    count = min(OUT_CHUNKS, units)
    sizes = [unit * ((units + k) // count) for k in range(count)]
    return [(sum(sizes[:k]), sizes[k]) for k in range(count)]


def kernel(
    cfg,
    len_ref,
    sink_ref,
    dest_hbm,
    logp_hbm,
    hidden_hbm,
    grad_hbm,
    wq_hbm,
    wkv_hbm,
    out_ref,
    loss_ref,
    dest_v,
    logp_v,
    hidden_v,
    grad_v,
    wq_v,
    wkv_raw,
    wkv_f,
    wkv_v,
    packed_v,
    send_kv,
    recv_kv,
    send_q,
    recv_q,
    note_send,
    note_recv,
    place_v,
    kvx,
    k4,
    v4,
    bias_v,
    coef_v,
    dk4,
    dv4,
    dq_v,
    kvg_b,
    kvg_f,
    halo_send,
    halo_recv,
    part,
    rs_recv,
    load_sem,
    kv_ss,
    kv_rs,
    q_ss,
    q_rs,
    note_ss,
    note_rs,
    edge_ss,
    edge_rs,
    halo_ss,
    halo_rs,
    rs_ss,
    rs_rs,
    ag_ss,
    ag_rs,
    own_sem,
):
    D, N, R, S, QC, KC, FEAT, HD, PC = cfg
    SENT = -(-(R // D + 1) // 8) * 8
    NC = QC // CHUNK
    KH = KC // (2 * HD)
    HPC = CHUNK // HD
    CPK = NC // KH
    BITS = log2(N)
    SLOTS = -(-(D * S) // LANES) * LANES
    scale = HD ** (-0.5)
    me = lax.axis_index("seq")
    hd = lax.axis_index("head")
    bounds = chunk_bounds(FEAT, N)

    loads = [
        pltpu.make_async_copy(dest_hbm, dest_v, load_sem.at[0]),
        pltpu.make_async_copy(hidden_hbm, hidden_v, load_sem.at[1]),
    ]

    def q_load(c):
        columns = pl.ds(pl.multiple_of(c * CHUNK, CHUNK), CHUNK)
        return pltpu.make_async_copy(wq_hbm.at[:, columns], wq_v.at[c], load_sem.at[5 + c])

    logp_load = pltpu.make_async_copy(logp_hbm, logp_v, load_sem.at[2])
    wkv_load = pltpu.make_async_copy(wkv_hbm, wkv_raw, load_sem.at[3])
    grad_load = pltpu.make_async_copy(grad_hbm, grad_v, load_sem.at[4])
    for load in loads:
        load.start()
    q_load(0).start()

    halo_recv[...] = jnp.zeros_like(halo_recv)
    kvx[0:WINDOW] = jnp.zeros((WINDOW, KC), BF16)
    recv_kv[:, S - 16 :, :] = jnp.zeros((D, 16, KC), BF16)
    recv_q[:, :, S - 16 :, :] = jnp.zeros((NC, D, 16, CHUNK), BF16)

    def peer_of(j):
        return lax.rem(me + j, D)

    def bit_of(b):
        return lax.rem(hd // (1 << b), 2)

    def partner_of(b):
        return hd + (1 - 2 * bit_of(b)) * (1 << b)

    barrier = pltpu.get_barrier_semaphore()

    def greet(j, _):
        pl.semaphore_signal(
            barrier, inc=1, device_id={"seq": peer_of(j)}, device_id_type=MESH
        )
        return 0

    lax.fori_loop(1, D, greet, 0)
    for b in range(BITS):
        pl.semaphore_signal(
            barrier, inc=1, device_id={"head": partner_of(b)}, device_id_type=MESH
        )

    rotation = (WINDOW // 2 - D // 2 * R) % PAIR_POSITIONS
    total = PC * PAIR_POSITIONS
    first = lax.rem(me * R - WINDOW + rotation + total, total)
    pair_a = first // PAIR_POSITIONS
    pair_b = lax.rem(pair_a + 1, PC)
    len_a = len_ref[pair_a]
    len_b = len_ref[pair_b]

    def segment_of(position):
        u = position + rotation
        u = jnp.where(u >= total, u - total, u)
        pair = lax.shift_right_arithmetic(u, jnp.full_like(u, log2(PAIR_POSITIONS)))
        within = u - pair * PAIR_POSITIONS
        limit = jnp.where(pair == pair_a, len_a, len_b)
        return 2 * pair + jnp.where(within >= limit, 1, 0)

    loads[0].wait()
    dest = dest_v[...]
    dev = lax.shift_right_arithmetic(dest, jnp.full_like(dest, log2(R)))
    DP = max(16, D)
    hot = jnp.where(dev == iota((DP, R), 0), 1.0, 0.0)
    upper = jnp.where(iota((R, R), 0) < iota((R, R), 1), 1.0, 0.0).astype(BF16)
    before = dot_nn(hot.astype(BF16), upper)
    within = jnp.sum(hot * before, axis=0, keepdims=True).astype(jnp.int32)
    pack = jnp.where(dev * S + within == iota((D * S, R), 0), 1.0, 0.0).astype(BF16)

    loads[1].wait()
    logp_load.start()
    wkv_load.start()
    for o in range(0, FEAT, 4 * LANES):
        w = min(4 * LANES, FEAT - o)
        packed_v[:, o : o + w] = dot_nt(pack, hidden_v[o : o + w, :]).astype(BF16)

    def note_copy(peer, slot):
        return pltpu.make_async_remote_copy(
            src_ref=note_send.at[peer],
            dst_ref=note_recv.at[slot],
            send_sem=note_ss.at[peer],
            recv_sem=note_rs.at[slot],
            device_id={"seq": peer},
            device_id_type=MESH,
        )

    def kv_copy(peer, slot):
        return pltpu.make_async_remote_copy(
            src_ref=send_kv.at[peer, pl.ds(0, SENT)],
            dst_ref=recv_kv.at[slot, pl.ds(0, SENT)],
            send_sem=kv_ss.at[peer],
            recv_sem=kv_rs.at[slot],
            device_id={"seq": peer},
            device_id_type=MESH,
        )

    def q_copy(c, peer, slot):
        return pltpu.make_async_remote_copy(
            src_ref=send_q.at[c, peer, pl.ds(0, SENT)],
            dst_ref=recv_q.at[c, slot, pl.ds(0, SENT)],
            send_sem=q_ss.at[c, peer],
            recv_sem=q_rs.at[c, slot],
            device_id={"seq": peer},
            device_id_type=MESH,
        )

    def each_peer(fn):
        def step(j, _):
            fn(peer_of(j))
            return 0

        lax.fori_loop(1, D, step, 0)

    def project(c, _):
        q_load(c).wait()
        send_q[c] = dot_nn(packed_v[...], wq_v[c]).astype(BF16).reshape(D, S, CHUNK)
        recv_q[c, me] = send_q[c, me]

        @pl.when(c == 1)
        def _():
            each_peer(lambda p: q_copy(c, p, me).start())

        return 0

    q_load(0).wait()
    for c in range(1, NC):
        q_load(c).start()
    grad_load.start()
    send_q[0] = dot_nn(packed_v[...], wq_v[0]).astype(BF16).reshape(D, S, CHUNK)
    pl.semaphore_wait(barrier, D - 1 + BITS)
    each_peer(lambda p: q_copy(0, p, me).start())
    recv_q[0, me] = send_q[0, me]

    place = hot * (dest - dev * R + 1).astype(F32)
    mine = jnp.where(me * S + within == iota((SLOTS, R), 0), 1.0, 0.0)
    places = dot_nt(place.astype(BF16), mine.astype(BF16))
    logp_load.wait()
    row_seg = segment_of(me * R + iota((1, R), 1))
    spread = jnp.where(row_seg == iota((LANES, R), 0), logp_v[...], 0.0)
    local_tot = jnp.sum(spread.T, axis=0, keepdims=True)
    for p in range(D):
        note_send[p, :, 0:SLOTS] = places[p : p + 1, :]
        note_send[p, :, SLOTS:] = local_tot
    each_peer(lambda p: note_copy(p, me).start())
    note_recv[me] = note_send[me]

    wkv_load.wait()
    UNI = FEAT // 10

    def untangle(b, _):
        rows = pl.multiple_of(b * UNI, 16)
        wkv_f[...] = wkv_raw[pl.ds(pl.multiple_of(b * UNI * KH, 16), UNI * KH), :].astype(F32)
        for h in range(KH):
            wkv_v[pl.ds(rows, UNI), h * 2 * HD : (h + 1) * 2 * HD] = wkv_f[
                pl.ds(h, UNI, stride=KH), :
            ].astype(BF16)
        return 0

    lax.fori_loop(0, FEAT // UNI, untangle, 0)
    send_kv[...] = dot_nn(packed_v[...], wkv_v[...]).astype(BF16).reshape(D, S, KC)
    each_peer(lambda p: kv_copy(p, me).start())
    recv_kv[me] = send_kv[me]

    lax.fori_loop(1, NC, project, 0)

    for r in range(R // WINDOW):
        base = me * R + r * WINDOW
        key_pos = base - WINDOW + iota((2 * WINDOW, 1), 0)
        query_pos = base + iota((1, WINDOW), 1)
        offset = query_pos - key_pos
        key_seg = segment_of(key_pos)
        query_seg = segment_of(query_pos)
        allowed = (
            (key_pos >= 0) & (offset >= 0) & (offset < WINDOW) & (key_seg == query_seg)
        )
        bias_v[r] = jnp.where(allowed, 0.0, NEG_FILL)

    each_peer(lambda p: note_copy(p, p).wait_recv())
    notes = jnp.sum(note_recv[...], axis=0)
    place_v[...] = jnp.where(
        iota((R, SLOTS), 0) + 1 == notes[:, 0:SLOTS].astype(jnp.int32), 1.0, 0.0
    ).astype(BF16)[:, 0 : D * S]
    seg_tot = notes[:, SLOTS:]
    lane = iota((1, LANES), 1)
    seg_len = jnp.ones((1, LANES), jnp.int32)
    for p in range(PC):
        seg_len = jnp.where(lane == 2 * p, len_ref[p], seg_len)
        seg_len = jnp.where(lane == 2 * p + 1, PAIR_POSITIONS - len_ref[p], seg_len)
    seg_len = seg_len.astype(F32)
    mean = seg_tot / seg_len
    margin = BETA * (mean - pltpu.roll(mean, LANES - 1, 1)) - GAMMA
    neg = -margin
    tail = jnp.exp(-jnp.abs(neg))
    loss = jnp.maximum(neg, 0.0) + jnp.log1p(tail)
    for p in range(PC):
        loss_ref[p] = jnp.sum(jnp.where(lane == 2 * p, loss, 0.0))
    weight = jnp.where(neg >= 0, 1.0 / (1.0 + tail), tail / (1.0 + tail)) * (BETA * LOSS_SCALE)
    even = (lane & 1) == 0
    coef = jnp.where(even, -weight, pltpu.roll(weight, 1, 1)) / seg_len
    col_seg = segment_of(me * R + iota((R, 1), 0))
    coef_v[...] = jnp.broadcast_to(
        jnp.sum(jnp.where(col_seg == iota((R, LANES), 1), coef, 0.0), axis=1, keepdims=True),
        (R, LANES),
    )

    dk4[...] = jnp.zeros_like(dk4)
    dv4[...] = jnp.zeros_like(dv4)

    each_peer(lambda p: kv_copy(p, p).wait_recv())
    if NC > 2:
        each_peer(lambda p: q_copy(2, p, me).start())
    kvx[WINDOW:] = dot_nn(place_v[...], recv_kv[...].reshape(D * S, KC)).astype(BF16)

    edge = pltpu.make_async_remote_copy(
        src_ref=kvx.at[pl.ds(R, WINDOW)],
        dst_ref=kvx.at[pl.ds(0, WINDOW)],
        send_sem=edge_ss,
        recv_sem=edge_rs,
        device_id={"seq": lax.rem(me + 1, D)},
        device_id_type=MESH,
    )

    @pl.when(me < D - 1)
    def _():
        edge.start()

    grad_load.wait()

    @pl.when(me > 0)
    def _():
        edge.wait_recv()

    low = iota((R + WINDOW, LANES), 1) < HD
    for h in range(KH):
        kv = kvx[:, h * 2 * HD : (h + 1) * 2 * HD].astype(F32)
        turned = pltpu.roll(kv, HD, 1)
        kk = jnp.where(low, kv, turned).astype(BF16)
        vv = jnp.where(low, turned, kv).astype(BF16)
        for g in range(CHUNK // LANES):
            k4[h, :, g * LANES : (g + 1) * LANES] = kk
            v4[h, :, g * LANES : (g + 1) * LANES] = vv

    head_of = lax.shift_right_arithmetic(
        iota((WINDOW, CHUNK), 1), jnp.full((WINDOW, CHUNK), log2(HD), jnp.int32)
    )

    def spread_heads(x):
        return jnp.concatenate(
            [jnp.where(head_of == g, x, 0.0).astype(BF16) for g in range(HPC)], axis=0
        )

    halo = pltpu.make_async_remote_copy(
        src_ref=halo_send,
        dst_ref=halo_recv,
        send_sem=halo_ss,
        recv_sem=halo_rs,
        device_id={"seq": lax.rem(me + D - 1, D)},
        device_id_type=MESH,
    )

    def fold(h, rows):
        folded = []
        for acc in (dk4, dv4):
            y = acc[h, rows, 0:LANES]
            for g in range(1, CHUNK // LANES):
                y = y + acc[h, rows, g * LANES : (g + 1) * LANES]
            folded.append(y + pltpu.roll(y, HD, 1))
        return jnp.where(low[rows], folded[0] * scale, folded[1])

    def attend(c, _):
        h = c // CPK
        each_peer(lambda p: q_copy(c, p, p).wait_recv())

        @pl.when(c + 3 < NC)
        def _():
            each_peer(lambda p: q_copy(c + 3, p, me).start())

        q_all = dot_nn(place_v[...], recv_q[c].reshape(D * S, CHUNK))
        g_all = grad_v[:, pl.ds(pl.multiple_of(c * CHUNK, CHUNK), CHUNK)].astype(F32)
        factor = coef_v[...]
        g_all = g_all * jnp.concatenate([factor] * (CHUNK // LANES), axis=1)
        sink = jnp.concatenate(
            [jnp.full((1, WINDOW), sink_ref[c * HPC + g], F32) for g in range(HPC)], axis=1
        )
        for r in range(R // WINDOW):
            rows = slice(r * WINDOW, (r + 1) * WINDOW)
            keys = slice(r * WINDOW, (r + 2) * WINDOW)
            qz = spread_heads(q_all[rows])
            gz = spread_heads(g_all[rows])
            kr = k4[h, keys, :]
            vr = v4[h, keys, :]
            bias = bias_v[r]
            masked = dot_nt(kr, qz) * scale + jnp.concatenate([bias] * HPC, axis=1)
            top = jnp.maximum(jnp.max(masked, axis=0, keepdims=True), sink)
            expo = jnp.exp(masked - top)
            denom = jnp.exp(sink - top) + jnp.sum(expo, axis=0, keepdims=True)
            probs = expo * (1.0 / denom)
            probs_b = probs.astype(BF16)
            prob_grad = dot_nt(vr, gz)
            row_dot = jnp.sum(probs_b.astype(F32) * prob_grad, axis=0, keepdims=True)
            score_grad = (probs * (prob_grad - row_dot)).astype(BF16)
            dk4[h, keys, :] += dot_nn(score_grad, qz)
            dv4[h, keys, :] += dot_nn(probs_b, gz)
            if r == 0:

                @pl.when(c == NC - 1)
                def _():
                    for k in range(KH):
                        halo_send[:, k * 2 * HD : (k + 1) * 2 * HD] = fold(
                            k, slice(0, WINDOW)
                        ).astype(BF16)

                @pl.when((c == NC - 1) & (me > 0))
                def _():
                    halo.start()

            wide = dot_tn(score_grad, kr)
            dq = jnp.where(head_of == 0, wide[0:WINDOW], 0.0)
            for g in range(1, HPC):
                dq = jnp.where(head_of == g, wide[g * WINDOW : (g + 1) * WINDOW], dq)
            dq_v[c, rows, :] = (dq * scale).astype(BF16)
        return 0

    lax.fori_loop(0, NC, attend, 0)

    for h in range(KH):
        cols = slice(h * 2 * HD, (h + 1) * 2 * HD)
        kvg_f[:, cols] = fold(h, slice(WINDOW, WINDOW + R))

    def ranges(s, n):
        off, size = bounds[n]
        order = list(range(BITS)) if n % 2 == 0 else list(reversed(range(BITS)))
        for t in range(s + 1):
            size //= 2
            bit = bit_of(order[t])
            keep = off + bit * size
            give = off + (1 - bit) * size
            off = keep
        return pl.multiple_of(keep, 16), pl.multiple_of(give, 16), size, partner_of(order[s])

    def landing(s, n):
        o, w = bounds[n]
        size = w >> (s + 1)
        return pl.ds(o + w - 2 * size, size)

    def rs_copy(s, n):
        keep, give, size, partner = ranges(s, n)
        return pltpu.make_async_remote_copy(
            src_ref=part.at[pl.ds(give, size)],
            dst_ref=rs_recv.at[landing(s, n)],
            send_sem=rs_ss.at[s, n],
            recv_sem=rs_rs.at[s, n],
            device_id={"head": partner},
            device_id_type=MESH,
        )

    def ag_copy(s, n, mine):
        keep, give, size, partner = ranges(s, n)
        rows = pl.ds(keep if mine else give, size)
        return pltpu.make_async_remote_copy(
            src_ref=(part if s == BITS - 1 else out_ref).at[rows],
            dst_ref=out_ref.at[rows],
            send_sem=ag_ss.at[s, n],
            recv_sem=ag_rs.at[s, n],
            device_id={"head": partner},
            device_id_type=MESH,
        )

    def own_copy(n):
        keep, give, size, partner = ranges(BITS - 1, n)
        rows = pl.ds(keep, size)
        return pltpu.make_async_copy(part.at[rows], out_ref.at[rows], own_sem.at[n])

    for n, (o, w) in enumerate(bounds):
        e = min(o + w, FEAT)
        acc = dot_nt(wq_v[0, o:e, :], dq_v[0])
        for c in range(1, NC):
            acc = acc + dot_nt(wq_v[c, o:e, :], dq_v[c])
        if n == 0:

            @pl.when(me < D - 1)
            def _():
                halo.wait_recv()

            kvg_b[0 : R - WINDOW] = kvg_f[0 : R - WINDOW].astype(BF16)
            kvg_b[R - WINDOW :] = (
                kvg_f[R - WINDOW :] + halo_recv[...].astype(F32)
            ).astype(BF16)
        acc = acc + dot_nt(wkv_v[o:e, :], kvg_b[...])
        part[o:e, :] = acc.astype(BF16)
        if o + w > e:
            part[e : o + w, :] = jnp.zeros((o + w - e, R), BF16)
        rs_copy(0, n).start()

    for s in range(BITS):
        for n in range(len(bounds)):
            rs_copy(s, n).wait_recv()
            keep, give, size, partner = ranges(s, n)
            added = part[pl.ds(keep, size), :].astype(F32) + rs_recv[landing(s, n), :].astype(F32)
            part[pl.ds(keep, size), :] = added.astype(BF16)
            if s < BITS - 1:
                rs_copy(s + 1, n).start()
            else:
                ag_copy(s, n, True).start()
                own_copy(n).start()

    for s in reversed(range(BITS)):
        for n in range(len(bounds)):
            ag_copy(s, n, False).wait_recv()
            if s == BITS - 1:
                own_copy(n).wait()
            if s > 0:
                ag_copy(s - 1, n, True).start()

    each_peer(lambda p: note_copy(p, me).wait_send())
    each_peer(lambda p: kv_copy(p, me).wait_send())
    for c in range(NC):
        each_peer(lambda p: q_copy(c, p, me).wait_send())

    @pl.when(me < D - 1)
    def _():
        edge.wait_send()

    @pl.when(me > 0)
    def _():
        halo.wait_send()

    for s in range(BITS):
        for n in range(len(bounds)):
            rs_copy(s, n).wait_send()
            ag_copy(s, n, True).wait_send()


def local(hidden, dest_pos, chosen_len, token_logp, head_grad, q_weight, key_value_weight, sinks):
    D, N = lax.axis_size("seq"), lax.axis_size("head")
    R, FEAT = hidden.shape
    HD = key_value_weight.shape[2] // 2
    KH = key_value_weight.shape[1]
    KC = KH * 2 * HD
    QC = q_weight.shape[1]
    PC = chosen_len.shape[0]
    S = -(-(R // D + 1) // 16) * 16
    NC = QC // CHUNK
    BITS = log2(N)
    SLOTS = -(-(D * S) // LANES) * LANES
    bounds = chunk_bounds(FEAT, N)
    NB = len(bounds)
    wide = bounds[-1][0] + bounds[-1][1]
    cfg = (D, N, R, S, QC, KC, FEAT, HD, PC)
    smem = pl.BlockSpec(memory_space=pltpu.SMEM)
    hbm = pl.BlockSpec(memory_space=pltpu.HBM)
    anywhere = pl.BlockSpec(memory_space=pl.ANY)
    dma = pltpu.SemaphoreType.DMA
    grad, loss = pl.pallas_call(
        functools.partial(kernel, cfg),
        out_shape=(
            pltpu.VMEM((wide, R), BF16),
            jax.ShapeDtypeStruct((PC,), F32),
        ),
        in_specs=[smem, smem, hbm, hbm, hbm, hbm, hbm, hbm],
        out_specs=(anywhere, smem),
        scratch_shapes=[
            pltpu.VMEM((1, R), jnp.int32),
            pltpu.VMEM((1, R), F32),
            pltpu.VMEM((FEAT, R), BF16),
            pltpu.VMEM((R, QC), BF16),
            pltpu.VMEM((NC, FEAT, CHUNK), BF16),
            pltpu.VMEM((FEAT * KH, 2 * HD), BF16),
            pltpu.VMEM((FEAT // 10 * KH, 2 * HD), F32),
            pltpu.VMEM((FEAT, KC), BF16),
            pltpu.VMEM((D * S, FEAT), BF16),
            pltpu.VMEM((D, S, KC), BF16),
            pltpu.VMEM((D, S, KC), BF16),
            pltpu.VMEM((NC, D, S, CHUNK), BF16),
            pltpu.VMEM((NC, D, S, CHUNK), BF16),
            pltpu.VMEM((D, 1, SLOTS + LANES), F32),
            pltpu.VMEM((D, 1, SLOTS + LANES), F32),
            pltpu.VMEM((R, D * S), BF16),
            pltpu.VMEM((R + WINDOW, KC), BF16),
            pltpu.VMEM((KH, R + WINDOW, CHUNK), BF16),
            pltpu.VMEM((KH, R + WINDOW, CHUNK), BF16),
            pltpu.VMEM((R // WINDOW, 2 * WINDOW, WINDOW), F32),
            pltpu.VMEM((R, LANES), F32),
            pltpu.VMEM((KH, R + WINDOW, CHUNK), F32),
            pltpu.VMEM((KH, R + WINDOW, CHUNK), F32),
            pltpu.VMEM((NC, R, CHUNK), BF16),
            pltpu.VMEM((R, KC), BF16),
            pltpu.VMEM((R, KC), F32),
            pltpu.VMEM((WINDOW, KC), BF16),
            pltpu.VMEM((WINDOW, KC), BF16),
            pltpu.VMEM((wide, R), BF16),
            pltpu.VMEM((wide, R), BF16),
            dma((5 + NC,)),
            dma((D,)),
            dma((D,)),
            dma((NC, D)),
            dma((NC, D)),
            dma((D,)),
            dma((D,)),
            dma,
            dma,
            dma,
            dma,
            dma((BITS, NB)),
            dma((BITS, NB)),
            dma((BITS, NB)),
            dma((BITS, NB)),
            dma((NB,)),
        ],
        compiler_params=pltpu.CompilerParams(
            collective_id=0, has_side_effects=True, vmem_limit_bytes=60 * 1024 * 1024
        ),
        name="preference_gradient",
    )(
        chosen_len,
        sinks,
        dest_pos.reshape(1, R),
        token_logp.reshape(1, R),
        hidden.T,
        head_grad,
        q_weight,
        key_value_weight.reshape(FEAT * KH, 2 * HD),
    )
    return grad[:FEAT].T, loss


def solution(mesh):
    placed = (
        P(("batch", "seq"), None),
        P(("batch", "seq")),
        P("batch"),
        P(("batch", "seq")),
        P(("batch", "seq"), "head"),
        P(None, "head"),
        P(None, "head", None),
        P("head"),
    )
    return jax.shard_map(
        local,
        mesh=mesh,
        in_specs=placed,
        out_specs=(P(("batch", "seq"), None), P("batch")),
        check_vma=False,
    )
```

```python
import functools

import jax
import jax.numpy as jnp
from jax import lax
from jax.experimental import pallas as pl
from jax.experimental.pallas import tpu as pltpu
from jax.sharding import PartitionSpec as P

WINDOW = 128
PAIR_POSITIONS = 512
BETA = 2.0
GAMMA = 1.0
LOSS_SCALE = 256.0
NEG_FILL = -1e30
LANES = 128
CHUNK = 256
OUT_CHUNKS = 10
AHEAD = 5
F32 = jnp.float32
BF16 = jnp.bfloat16
MESH = pl.DeviceIdType.MESH


def dot_nn(a, b):
    return lax.dot_general(a, b, (((1,), (0,)), ((), ())), preferred_element_type=F32)


def dot_nt(a, b):
    return lax.dot_general(a, b, (((1,), (1,)), ((), ())), preferred_element_type=F32)


def dot_tn(a, b):
    return lax.dot_general(a, b, (((0,), (0,)), ((), ())), preferred_element_type=F32)


def iota(shape, dim):
    return lax.broadcasted_iota(jnp.int32, shape, dim)


def log2(n):
    assert n & (n - 1) == 0
    return n.bit_length() - 1


def chunk_bounds(feat, n):
    unit = 16 * n
    units = -(-feat // unit)
    count = min(OUT_CHUNKS, units)
    sizes = [unit * ((units + k) // count) for k in range(count)]
    return [(sum(sizes[:k]), sizes[k]) for k in range(count)]


def kernel(
    cfg,
    len_hbm,
    sink_hbm,
    dest_hbm,
    logp_hbm,
    hidden_hbm,
    grad_hbm,
    wq_hbm,
    wkv_hbm,
    out_ref,
    loss_hbm,
    len_ref,
    sink_ref,
    loss_ref,
    dest_v,
    logp_v,
    hidden_v,
    grad_v,
    wq_v,
    wkv_raw,
    wkv_f,
    wkv_v,
    packed_v,
    send_kv,
    recv_kv,
    send_q,
    recv_q,
    note_send,
    note_recv,
    place_v,
    kvx,
    k4,
    v4,
    bias_v,
    coef_v,
    dk4,
    dv4,
    dq_v,
    kvg_b,
    kvg_f,
    halo_send,
    halo_recv,
    part,
    rs_recv,
    load_sem,
    kv_ss,
    kv_rs,
    q_ss,
    q_rs,
    note_ss,
    note_rs,
    edge_ss,
    edge_rs,
    halo_ss,
    halo_rs,
    rs_ss,
    rs_rs,
    ag_ss,
    ag_rs,
    own_sem,
    small_sem,
):
    D, N, R, S, QC, KC, FEAT, HD, PC = cfg
    SENT = -(-(R // D + 1) // 8) * 8
    NC = QC // CHUNK
    KH = KC // (2 * HD)
    HPC = CHUNK // HD
    CPK = NC // KH
    BITS = log2(N)
    SLOTS = -(-(D * S) // LANES) * LANES
    scale = HD ** (-0.5)
    me = lax.axis_index("seq")
    hd = lax.axis_index("head")
    bounds = chunk_bounds(FEAT, N)

    loads = [
        pltpu.make_async_copy(dest_hbm, dest_v, load_sem.at[0]),
        pltpu.make_async_copy(hidden_hbm, hidden_v, load_sem.at[1]),
    ]

    def q_load(c):
        columns = pl.ds(pl.multiple_of(c * CHUNK, CHUNK), CHUNK)
        return pltpu.make_async_copy(wq_hbm.at[:, columns], wq_v.at[c], load_sem.at[5 + c])

    logp_load = pltpu.make_async_copy(logp_hbm, logp_v, load_sem.at[2])
    wkv_load = pltpu.make_async_copy(wkv_hbm, wkv_raw, load_sem.at[3])
    grad_load = pltpu.make_async_copy(grad_hbm, grad_v, load_sem.at[4])
    len_load = pltpu.make_async_copy(len_hbm, len_ref, small_sem.at[0])
    sink_load = pltpu.make_async_copy(sink_hbm, sink_ref, small_sem.at[1])
    loss_store = pltpu.make_async_copy(loss_ref, loss_hbm, small_sem.at[2])
    for load in loads:
        load.start()
    q_load(0).start()
    len_load.start()
    sink_load.start()

    halo_recv[...] = jnp.zeros_like(halo_recv)
    kvx[0:WINDOW] = jnp.zeros((WINDOW, KC), BF16)
    recv_kv[:, S - 16 :, :] = jnp.zeros((D, 16, KC), BF16)
    recv_q[:, :, S - 16 :, :] = jnp.zeros((NC, D, 16, CHUNK), BF16)

    def peer_of(j):
        return lax.rem(me + j, D)

    def bit_of(b):
        return lax.rem(hd // (1 << b), 2)

    def partner_of(b):
        return hd + (1 - 2 * bit_of(b)) * (1 << b)

    barrier = pltpu.get_barrier_semaphore()

    def greet(j, _):
        pl.semaphore_signal(
            barrier, inc=1, device_id={"seq": peer_of(j)}, device_id_type=MESH
        )
        return 0

    lax.fori_loop(1, D, greet, 0)
    for b in range(BITS):
        pl.semaphore_signal(
            barrier, inc=1, device_id={"head": partner_of(b)}, device_id_type=MESH
        )

    loads[0].wait()
    dest = dest_v[...]
    dev = lax.shift_right_arithmetic(dest, jnp.full_like(dest, log2(R)))
    DP = max(16, D)
    hot = jnp.where(dev == iota((DP, R), 0), 1.0, 0.0)
    upper = jnp.where(iota((R, R), 0) < iota((R, R), 1), 1.0, 0.0).astype(BF16)
    before = dot_nn(hot.astype(BF16), upper)
    within = jnp.sum(hot * before, axis=0, keepdims=True).astype(jnp.int32)
    pack = jnp.where(dev * S + within == iota((D * S, R), 0), 1.0, 0.0).astype(BF16)

    loads[1].wait()
    logp_load.start()
    wkv_load.start()
    for o in range(0, FEAT, 4 * LANES):
        w = min(4 * LANES, FEAT - o)
        packed_v[:, o : o + w] = dot_nt(pack, hidden_v[o : o + w, :]).astype(BF16)

    def note_copy(peer, slot):
        return pltpu.make_async_remote_copy(
            src_ref=note_send.at[peer],
            dst_ref=note_recv.at[slot],
            send_sem=note_ss.at[peer],
            recv_sem=note_rs.at[slot],
            device_id={"seq": peer},
            device_id_type=MESH,
        )

    def kv_copy(peer, slot):
        return pltpu.make_async_remote_copy(
            src_ref=send_kv.at[peer, pl.ds(0, SENT)],
            dst_ref=recv_kv.at[slot, pl.ds(0, SENT)],
            send_sem=kv_ss.at[peer],
            recv_sem=kv_rs.at[slot],
            device_id={"seq": peer},
            device_id_type=MESH,
        )

    def q_copy(c, peer, slot):
        return pltpu.make_async_remote_copy(
            src_ref=send_q.at[c, peer, pl.ds(0, SENT)],
            dst_ref=recv_q.at[c, slot, pl.ds(0, SENT)],
            send_sem=q_ss.at[c, peer],
            recv_sem=q_rs.at[c, slot],
            device_id={"seq": peer},
            device_id_type=MESH,
        )

    def each_peer(fn):
        def step(j, _):
            fn(peer_of(j))
            return 0

        lax.fori_loop(1, D, step, 0)

    def project(c, _):
        q_load(c).wait()
        send_q[c] = dot_nn(packed_v[...], wq_v[c]).astype(BF16).reshape(D, S, CHUNK)
        recv_q[c, me] = send_q[c, me]

        @pl.when(c == 1)
        def _():
            each_peer(lambda p: q_copy(c, p, me).start())

        return 0

    q_load(0).wait()
    for c in range(1, NC):
        q_load(c).start()
    grad_load.start()
    send_q[0] = dot_nn(packed_v[...], wq_v[0]).astype(BF16).reshape(D, S, CHUNK)
    pl.semaphore_wait(barrier, D - 1 + BITS)
    each_peer(lambda p: q_copy(0, p, me).start())
    recv_q[0, me] = send_q[0, me]

    place = hot * (dest - dev * R + 1).astype(F32)
    mine = jnp.where(me * S + within == iota((SLOTS, R), 0), 1.0, 0.0)
    places = dot_nt(place.astype(BF16), mine.astype(BF16))
    len_load.wait()
    rotation = (WINDOW // 2 - D // 2 * R) % PAIR_POSITIONS
    total = PC * PAIR_POSITIONS
    first = lax.rem(me * R - WINDOW + rotation + total, total)
    pair_a = first // PAIR_POSITIONS
    pair_b = lax.rem(pair_a + 1, PC)
    len_a = len_ref[pair_a]
    len_b = len_ref[pair_b]

    def segment_of(position):
        u = position + rotation
        u = jnp.where(u >= total, u - total, u)
        pair = lax.shift_right_arithmetic(u, jnp.full_like(u, log2(PAIR_POSITIONS)))
        within = u - pair * PAIR_POSITIONS
        limit = jnp.where(pair == pair_a, len_a, len_b)
        return 2 * pair + jnp.where(within >= limit, 1, 0)

    logp_load.wait()
    row_seg = segment_of(me * R + iota((1, R), 1))
    spread = jnp.where(row_seg == iota((LANES, R), 0), logp_v[...], 0.0)
    local_tot = jnp.sum(spread.T, axis=0, keepdims=True)
    for p in range(D):
        note_send[p, :, 0:SLOTS] = places[p : p + 1, :]
        note_send[p, :, SLOTS:] = local_tot
    each_peer(lambda p: note_copy(p, me).start())
    note_recv[me] = note_send[me]

    wkv_load.wait()
    UNI = FEAT // 10

    def untangle(b, _):
        rows = pl.multiple_of(b * UNI, 16)
        wkv_f[...] = wkv_raw[pl.ds(pl.multiple_of(b * UNI * KH, 16), UNI * KH), :].astype(F32)
        for h in range(KH):
            wkv_v[pl.ds(rows, UNI), h * 2 * HD : (h + 1) * 2 * HD] = wkv_f[
                pl.ds(h, UNI, stride=KH), :
            ].astype(BF16)
        return 0

    lax.fori_loop(0, FEAT // UNI, untangle, 0)
    send_kv[...] = dot_nn(packed_v[...], wkv_v[...]).astype(BF16).reshape(D, S, KC)
    each_peer(lambda p: kv_copy(p, me).start())
    recv_kv[me] = send_kv[me]

    lax.fori_loop(1, NC, project, 0)

    for r in range(R // WINDOW):
        base = me * R + r * WINDOW
        key_pos = base - WINDOW + iota((2 * WINDOW, 1), 0)
        query_pos = base + iota((1, WINDOW), 1)
        offset = query_pos - key_pos
        key_seg = segment_of(key_pos)
        query_seg = segment_of(query_pos)
        allowed = (
            (key_pos >= 0) & (offset >= 0) & (offset < WINDOW) & (key_seg == query_seg)
        )
        bias_v[r] = jnp.where(allowed, 0.0, NEG_FILL)

    each_peer(lambda p: note_copy(p, p).wait_recv())
    notes = jnp.sum(note_recv[...], axis=0)
    place_v[...] = jnp.where(
        iota((R, SLOTS), 0) + 1 == notes[:, 0:SLOTS].astype(jnp.int32), 1.0, 0.0
    ).astype(BF16)[:, 0 : D * S]
    seg_tot = notes[:, SLOTS:]
    lane = iota((1, LANES), 1)
    seg_len = jnp.ones((1, LANES), jnp.int32)
    for p in range(PC):
        seg_len = jnp.where(lane == 2 * p, len_ref[p], seg_len)
        seg_len = jnp.where(lane == 2 * p + 1, PAIR_POSITIONS - len_ref[p], seg_len)
    seg_len = seg_len.astype(F32)
    mean = seg_tot / seg_len
    margin = BETA * (mean - pltpu.roll(mean, LANES - 1, 1)) - GAMMA
    neg = -margin
    tail = jnp.exp(-jnp.abs(neg))
    loss = jnp.maximum(neg, 0.0) + jnp.log1p(tail)
    for p in range(PC):
        loss_ref[p] = jnp.sum(jnp.where(lane == 2 * p, loss, 0.0))
    loss_store.start()
    weight = jnp.where(neg >= 0, 1.0 / (1.0 + tail), tail / (1.0 + tail)) * (BETA * LOSS_SCALE)
    even = (lane & 1) == 0
    coef = jnp.where(even, -weight, pltpu.roll(weight, 1, 1)) / seg_len
    col_seg = segment_of(me * R + iota((R, 1), 0))
    coef_v[...] = jnp.broadcast_to(
        jnp.sum(jnp.where(col_seg == iota((R, LANES), 1), coef, 0.0), axis=1, keepdims=True),
        (R, LANES),
    )

    dk4[...] = jnp.zeros_like(dk4)
    dv4[...] = jnp.zeros_like(dv4)

    each_peer(lambda p: kv_copy(p, p).wait_recv())
    if NC > 2:
        each_peer(lambda p: q_copy(2, p, me).start())
    kvx[WINDOW:] = dot_nn(place_v[...], recv_kv[...].reshape(D * S, KC)).astype(BF16)

    edge = pltpu.make_async_remote_copy(
        src_ref=kvx.at[pl.ds(R, WINDOW)],
        dst_ref=kvx.at[pl.ds(0, WINDOW)],
        send_sem=edge_ss,
        recv_sem=edge_rs,
        device_id={"seq": lax.rem(me + 1, D)},
        device_id_type=MESH,
    )

    @pl.when(me < D - 1)
    def _():
        edge.start()

    grad_load.wait()

    @pl.when(me > 0)
    def _():
        edge.wait_recv()

    low = iota((R + WINDOW, LANES), 1) < HD
    for h in range(KH):
        kv = kvx[:, h * 2 * HD : (h + 1) * 2 * HD].astype(F32)
        turned = pltpu.roll(kv, HD, 1)
        kk = jnp.where(low, kv, turned).astype(BF16)
        vv = jnp.where(low, turned, kv).astype(BF16)
        for g in range(CHUNK // LANES):
            k4[h, :, g * LANES : (g + 1) * LANES] = kk
            v4[h, :, g * LANES : (g + 1) * LANES] = vv

    head_of = lax.shift_right_arithmetic(
        iota((WINDOW, CHUNK), 1), jnp.full((WINDOW, CHUNK), log2(HD), jnp.int32)
    )

    def spread_heads(x):
        return jnp.concatenate(
            [jnp.where(head_of == g, x, 0.0).astype(BF16) for g in range(HPC)], axis=0
        )

    halo = pltpu.make_async_remote_copy(
        src_ref=halo_send,
        dst_ref=halo_recv,
        send_sem=halo_ss,
        recv_sem=halo_rs,
        device_id={"seq": lax.rem(me + D - 1, D)},
        device_id_type=MESH,
    )

    def fold(h, rows):
        folded = []
        for acc in (dk4, dv4):
            y = acc[h, rows, 0:LANES]
            for g in range(1, CHUNK // LANES):
                y = y + acc[h, rows, g * LANES : (g + 1) * LANES]
            folded.append(y + pltpu.roll(y, HD, 1))
        return jnp.where(low[rows], folded[0] * scale, folded[1])

    def attend(c, _):
        h = c // CPK
        each_peer(lambda p: q_copy(c, p, p).wait_recv())

        @pl.when(c + 3 < NC)
        def _():
            each_peer(lambda p: q_copy(c + 3, p, me).start())

        q_all = dot_nn(place_v[...], recv_q[c].reshape(D * S, CHUNK))
        g_all = grad_v[:, pl.ds(pl.multiple_of(c * CHUNK, CHUNK), CHUNK)].astype(F32)
        factor = coef_v[...]
        g_all = g_all * jnp.concatenate([factor] * (CHUNK // LANES), axis=1)
        sink = jnp.concatenate(
            [jnp.full((1, WINDOW), sink_ref[c * HPC + g], F32) for g in range(HPC)], axis=1
        )
        for r in range(R // WINDOW):
            rows = slice(r * WINDOW, (r + 1) * WINDOW)
            keys = slice(r * WINDOW, (r + 2) * WINDOW)
            qz = spread_heads(q_all[rows])
            gz = spread_heads(g_all[rows])
            kr = k4[h, keys, :]
            vr = v4[h, keys, :]
            bias = bias_v[r]
            masked = dot_nt(kr, qz) * scale + jnp.concatenate([bias] * HPC, axis=1)
            top = jnp.maximum(jnp.max(masked, axis=0, keepdims=True), sink)
            expo = jnp.exp(masked - top)
            denom = jnp.exp(sink - top) + jnp.sum(expo, axis=0, keepdims=True)
            probs = expo * (1.0 / denom)
            probs_b = probs.astype(BF16)
            prob_grad = dot_nt(vr, gz)
            row_dot = jnp.sum(probs_b.astype(F32) * prob_grad, axis=0, keepdims=True)
            score_grad = (probs * (prob_grad - row_dot)).astype(BF16)
            dk4[h, keys, :] += dot_nn(score_grad, qz)
            dv4[h, keys, :] += dot_nn(probs_b, gz)
            if r == 0:

                @pl.when(c == NC - 1)
                def _():
                    for k in range(KH):
                        halo_send[:, k * 2 * HD : (k + 1) * 2 * HD] = fold(
                            k, slice(0, WINDOW)
                        ).astype(BF16)

                @pl.when((c == NC - 1) & (me > 0))
                def _():
                    halo.start()

            wide = dot_tn(score_grad, kr)
            dq = jnp.where(head_of == 0, wide[0:WINDOW], 0.0)
            for g in range(1, HPC):
                dq = jnp.where(head_of == g, wide[g * WINDOW : (g + 1) * WINDOW], dq)
            dq_v[c, rows, :] = (dq * scale).astype(BF16)
        return 0

    sink_load.wait()
    lax.fori_loop(0, NC, attend, 0)

    for h in range(KH):
        cols = slice(h * 2 * HD, (h + 1) * 2 * HD)
        kvg_f[:, cols] = fold(h, slice(WINDOW, WINDOW + R))

    def ranges(s, n):
        off, size = bounds[n]
        order = list(range(BITS)) if n % 2 == 0 else list(reversed(range(BITS)))
        for t in range(s + 1):
            size //= 2
            bit = bit_of(order[t])
            keep = off + bit * size
            give = off + (1 - bit) * size
            off = keep
        return pl.multiple_of(keep, 16), pl.multiple_of(give, 16), size, partner_of(order[s])

    def landing(s, n):
        o, w = bounds[n]
        size = w >> (s + 1)
        return pl.ds(o + w - 2 * size, size)

    def rs_copy(s, n):
        keep, give, size, partner = ranges(s, n)
        return pltpu.make_async_remote_copy(
            src_ref=part.at[pl.ds(give, size)],
            dst_ref=rs_recv.at[landing(s, n)],
            send_sem=rs_ss.at[s, n],
            recv_sem=rs_rs.at[s, n],
            device_id={"head": partner},
            device_id_type=MESH,
        )

    def ag_copy(s, n, mine):
        keep, give, size, partner = ranges(s, n)
        rows = pl.ds(keep if mine else give, size)
        return pltpu.make_async_remote_copy(
            src_ref=(part if s == BITS - 1 else out_ref).at[rows],
            dst_ref=out_ref.at[rows],
            send_sem=ag_ss.at[s, n],
            recv_sem=ag_rs.at[s, n],
            device_id={"head": partner},
            device_id_type=MESH,
        )

    def own_copy(n):
        keep, give, size, partner = ranges(BITS - 1, n)
        rows = pl.ds(keep, size)
        return pltpu.make_async_copy(part.at[rows], out_ref.at[rows], own_sem.at[n])

    def query_part(n):
        o, w = bounds[n]
        e = min(o + w, FEAT)
        acc = dot_nt(wq_v[0, o:e, :], dq_v[0])
        for c in range(1, NC):
            acc = acc + dot_nt(wq_v[c, o:e, :], dq_v[c])
        return acc

    early = [query_part(n) for n in range(AHEAD)]

    @pl.when(me < D - 1)
    def _():
        halo.wait_recv()

    kvg_b[0 : R - WINDOW] = kvg_f[0 : R - WINDOW].astype(BF16)
    kvg_b[R - WINDOW :] = (kvg_f[R - WINDOW :] + halo_recv[...].astype(F32)).astype(BF16)
    for n, (o, w) in enumerate(bounds):
        e = min(o + w, FEAT)
        acc = early[n] if n < AHEAD else query_part(n)
        acc = acc + dot_nt(wkv_v[o:e, :], kvg_b[...])
        part[o:e, :] = acc.astype(BF16)
        if o + w > e:
            part[e : o + w, :] = jnp.zeros((o + w - e, R), BF16)
        rs_copy(0, n).start()

    for s in range(BITS):
        for n in range(len(bounds)):
            rs_copy(s, n).wait_recv()
            keep, give, size, partner = ranges(s, n)
            added = part[pl.ds(keep, size), :].astype(F32) + rs_recv[landing(s, n), :].astype(F32)
            part[pl.ds(keep, size), :] = added.astype(BF16)
            if s < BITS - 1:
                rs_copy(s + 1, n).start()
            else:
                ag_copy(s, n, True).start()
                own_copy(n).start()

    for s in reversed(range(BITS)):
        for n in range(len(bounds)):
            ag_copy(s, n, False).wait_recv()
            if s == BITS - 1:
                own_copy(n).wait()
            if s > 0:
                ag_copy(s - 1, n, True).start()

    each_peer(lambda p: note_copy(p, me).wait_send())
    each_peer(lambda p: kv_copy(p, me).wait_send())
    for c in range(NC):
        each_peer(lambda p: q_copy(c, p, me).wait_send())

    @pl.when(me < D - 1)
    def _():
        edge.wait_send()

    @pl.when(me > 0)
    def _():
        halo.wait_send()

    for s in range(BITS):
        for n in range(len(bounds)):
            rs_copy(s, n).wait_send()
            ag_copy(s, n, True).wait_send()
    loss_store.wait()


def local(hidden, dest_pos, chosen_len, token_logp, head_grad, q_weight, key_value_weight, sinks):
    D, N = lax.axis_size("seq"), lax.axis_size("head")
    R, FEAT = hidden.shape
    HD = key_value_weight.shape[2] // 2
    KH = key_value_weight.shape[1]
    KC = KH * 2 * HD
    QC = q_weight.shape[1]
    PC = chosen_len.shape[0]
    S = -(-(R // D + 1) // 16) * 16
    NC = QC // CHUNK
    BITS = log2(N)
    SLOTS = -(-(D * S) // LANES) * LANES
    bounds = chunk_bounds(FEAT, N)
    NB = len(bounds)
    wide = bounds[-1][0] + bounds[-1][1]
    cfg = (D, N, R, S, QC, KC, FEAT, HD, PC)
    hbm = pl.BlockSpec(memory_space=pltpu.HBM)
    anywhere = pl.BlockSpec(memory_space=pl.ANY)
    dma = pltpu.SemaphoreType.DMA
    grad, loss = pl.pallas_call(
        functools.partial(kernel, cfg),
        out_shape=(
            pltpu.VMEM((wide, R), BF16),
            jax.ShapeDtypeStruct((PC,), F32),
        ),
        in_specs=[hbm] * 8,
        out_specs=(anywhere, hbm),
        scratch_shapes=[
            pltpu.SMEM((PC,), jnp.int32),
            pltpu.SMEM(sinks.shape, F32),
            pltpu.SMEM((PC,), F32),
            pltpu.VMEM((1, R), jnp.int32),
            pltpu.VMEM((1, R), F32),
            pltpu.VMEM((FEAT, R), BF16),
            pltpu.VMEM((R, QC), BF16),
            pltpu.VMEM((NC, FEAT, CHUNK), BF16),
            pltpu.VMEM((FEAT * KH, 2 * HD), BF16),
            pltpu.VMEM((FEAT // 10 * KH, 2 * HD), F32),
            pltpu.VMEM((FEAT, KC), BF16),
            pltpu.VMEM((D * S, FEAT), BF16),
            pltpu.VMEM((D, S, KC), BF16),
            pltpu.VMEM((D, S, KC), BF16),
            pltpu.VMEM((NC, D, S, CHUNK), BF16),
            pltpu.VMEM((NC, D, S, CHUNK), BF16),
            pltpu.VMEM((D, 1, SLOTS + LANES), F32),
            pltpu.VMEM((D, 1, SLOTS + LANES), F32),
            pltpu.VMEM((R, D * S), BF16),
            pltpu.VMEM((R + WINDOW, KC), BF16),
            pltpu.VMEM((KH, R + WINDOW, CHUNK), BF16),
            pltpu.VMEM((KH, R + WINDOW, CHUNK), BF16),
            pltpu.VMEM((R // WINDOW, 2 * WINDOW, WINDOW), F32),
            pltpu.VMEM((R, LANES), F32),
            pltpu.VMEM((KH, R + WINDOW, CHUNK), F32),
            pltpu.VMEM((KH, R + WINDOW, CHUNK), F32),
            pltpu.VMEM((NC, R, CHUNK), BF16),
            pltpu.VMEM((R, KC), BF16),
            pltpu.VMEM((R, KC), F32),
            pltpu.VMEM((WINDOW, KC), BF16),
            pltpu.VMEM((WINDOW, KC), BF16),
            pltpu.VMEM((wide, R), BF16),
            pltpu.VMEM((wide, R), BF16),
            dma((5 + NC,)),
            dma((D,)),
            dma((D,)),
            dma((NC, D)),
            dma((NC, D)),
            dma((D,)),
            dma((D,)),
            dma,
            dma,
            dma,
            dma,
            dma((BITS, NB)),
            dma((BITS, NB)),
            dma((BITS, NB)),
            dma((BITS, NB)),
            dma((NB,)),
            dma((3,)),
        ],
        compiler_params=pltpu.CompilerParams(
            collective_id=0, has_side_effects=True, vmem_limit_bytes=60 * 1024 * 1024
        ),
        name="preference_gradient",
    )(
        chosen_len,
        sinks,
        dest_pos.reshape(1, R),
        token_logp.reshape(1, R),
        hidden.T,
        head_grad,
        q_weight,
        key_value_weight.reshape(FEAT * KH, 2 * HD),
    )
    return grad[:FEAT].T, loss


def solution(mesh):
    placed = (
        P(("batch", "seq"), None),
        P(("batch", "seq")),
        P("batch"),
        P(("batch", "seq")),
        P(("batch", "seq"), "head"),
        P(None, "head"),
        P(None, "head", None),
        P("head"),
    )
    return jax.shard_map(
        local,
        mesh=mesh,
        in_specs=placed,
        out_specs=(P(("batch", "seq"), None), P("batch")),
        check_vma=False,
    )
```

```python
import functools

import jax
import jax.numpy as jnp
from jax import lax
from jax.experimental import pallas as pl
from jax.experimental.pallas import tpu as pltpu
from jax.sharding import PartitionSpec as P

WINDOW = 128
PAIR_POSITIONS = 512
BETA = 2.0
GAMMA = 1.0
LOSS_SCALE = 256.0
NEG_FILL = -1e30
LANES = 128
CHUNK = 256
OUT_CHUNKS = 6
AHEAD = 3
F32 = jnp.float32
BF16 = jnp.bfloat16
MESH = pl.DeviceIdType.MESH


def dot_nn(a, b):
    return lax.dot_general(a, b, (((1,), (0,)), ((), ())), preferred_element_type=F32)


def dot_nt(a, b):
    return lax.dot_general(a, b, (((1,), (1,)), ((), ())), preferred_element_type=F32)


def dot_tn(a, b):
    return lax.dot_general(a, b, (((0,), (0,)), ((), ())), preferred_element_type=F32)


def iota(shape, dim):
    return lax.broadcasted_iota(jnp.int32, shape, dim)


def log2(n):
    assert n & (n - 1) == 0
    return n.bit_length() - 1


def chunk_bounds(feat, n):
    unit = 16 * n
    units = -(-feat // unit)
    count = min(OUT_CHUNKS, units)
    sizes = [unit * ((units + k) // count) for k in range(count)]
    return [(sum(sizes[:k]), sizes[k]) for k in range(count)]


def kernel(
    cfg,
    len_hbm,
    sink_hbm,
    dest_hbm,
    logp_hbm,
    hidden_hbm,
    grad_hbm,
    wq_hbm,
    wkv_hbm,
    out_ref,
    loss_hbm,
    len_ref,
    sink_ref,
    loss_ref,
    dest_v,
    logp_v,
    hidden_v,
    grad_v,
    wq_v,
    wkv_raw,
    wkv_f,
    wkv_v,
    packed_v,
    send_kv,
    recv_kv,
    send_q,
    recv_q,
    note_send,
    note_recv,
    xkv_send,
    xkv_recv,
    xq_send,
    xq_recv,
    place_v,
    kvx,
    k4,
    v4,
    bias_v,
    coef_v,
    dk4,
    dv4,
    dq_v,
    kvg_b,
    kvg_f,
    halo_send,
    halo_recv,
    part,
    rs_recv,
    load_sem,
    kv_ss,
    kv_rs,
    q_ss,
    q_rs,
    note_ss,
    note_rs,
    edge_ss,
    edge_rs,
    halo_ss,
    halo_rs,
    rs_ss,
    rs_rs,
    ag_ss,
    ag_rs,
    own_sem,
    small_sem,
    xkv_ss,
    xkv_rs,
    xq_ss,
    xq_rs,
):
    D, N, R, S, QC, KC, FEAT, HD, PC = cfg
    TRIM = R // D % 16 == 0
    SENT = R // D if TRIM else -(-(R // D + 1) // 8) * 8
    NC = QC // CHUNK
    KH = KC // (2 * HD)
    HPC = CHUNK // HD
    CPK = NC // KH
    BITS = log2(N)
    SLOTS = -(-(D * S) // LANES) * LANES
    scale = HD ** (-0.5)
    me = lax.axis_index("seq")
    hd = lax.axis_index("head")
    bounds = chunk_bounds(FEAT, N)

    loads = [
        pltpu.make_async_copy(dest_hbm, dest_v, load_sem.at[0]),
        pltpu.make_async_copy(hidden_hbm, hidden_v, load_sem.at[1]),
    ]

    def q_load(c):
        columns = pl.ds(pl.multiple_of(c * CHUNK, CHUNK), CHUNK)
        return pltpu.make_async_copy(wq_hbm.at[:, columns], wq_v.at[c], load_sem.at[5 + c])

    logp_load = pltpu.make_async_copy(logp_hbm, logp_v, load_sem.at[2])
    wkv_load = pltpu.make_async_copy(wkv_hbm, wkv_raw, load_sem.at[3])
    grad_load = pltpu.make_async_copy(grad_hbm, grad_v, load_sem.at[4])
    len_load = pltpu.make_async_copy(len_hbm, len_ref, small_sem.at[0])
    sink_load = pltpu.make_async_copy(sink_hbm, sink_ref, small_sem.at[1])
    loss_store = pltpu.make_async_copy(loss_ref, loss_hbm, small_sem.at[2])
    for load in loads:
        load.start()
    q_load(0).start()
    len_load.start()
    sink_load.start()

    halo_recv[...] = jnp.zeros_like(halo_recv)
    kvx[0:WINDOW] = jnp.zeros((WINDOW, KC), BF16)
    recv_kv[:, S - 16 :, :] = jnp.zeros((D, 16, KC), BF16)
    recv_q[:, :, S - 16 :, :] = jnp.zeros((NC, D, 16, CHUNK), BF16)

    def peer_of(j):
        return lax.rem(me + j, D)

    def bit_of(b):
        return lax.rem(hd // (1 << b), 2)

    def partner_of(b):
        return hd + (1 - 2 * bit_of(b)) * (1 << b)

    barrier = pltpu.get_barrier_semaphore()

    def greet(j, _):
        pl.semaphore_signal(
            barrier, inc=1, device_id={"seq": peer_of(j)}, device_id_type=MESH
        )
        return 0

    lax.fori_loop(1, D, greet, 0)
    for b in range(BITS):
        pl.semaphore_signal(
            barrier, inc=1, device_id={"head": partner_of(b)}, device_id_type=MESH
        )

    loads[0].wait()
    dest = dest_v[...]
    dev = lax.shift_right_arithmetic(dest, jnp.full_like(dest, log2(R)))
    DP = max(16, D)
    hot = jnp.where(dev == iota((DP, R), 0), 1.0, 0.0)
    upper = jnp.where(iota((R, R), 0) < iota((R, R), 1), 1.0, 0.0).astype(BF16)
    before = dot_nn(hot.astype(BF16), upper)
    within = jnp.sum(hot * before, axis=0, keepdims=True).astype(jnp.int32)
    pack = jnp.where(dev * S + within == iota((D * S, R), 0), 1.0, 0.0).astype(BF16)

    loads[1].wait()
    logp_load.start()
    wkv_load.start()
    for o in range(0, FEAT, 4 * LANES):
        w = min(4 * LANES, FEAT - o)
        packed_v[:, o : o + w] = dot_nt(pack, hidden_v[o : o + w, :]).astype(BF16)

    def note_copy(peer, slot):
        return pltpu.make_async_remote_copy(
            src_ref=note_send.at[peer],
            dst_ref=note_recv.at[slot],
            send_sem=note_ss.at[peer],
            recv_sem=note_rs.at[slot],
            device_id={"seq": peer},
            device_id_type=MESH,
        )

    def kv_copy(peer, slot):
        return pltpu.make_async_remote_copy(
            src_ref=send_kv.at[peer, pl.ds(0, SENT)],
            dst_ref=recv_kv.at[slot, pl.ds(0, SENT)],
            send_sem=kv_ss.at[peer],
            recv_sem=kv_rs.at[slot],
            device_id={"seq": peer},
            device_id_type=MESH,
        )

    def q_copy(c, peer, slot):
        return pltpu.make_async_remote_copy(
            src_ref=send_q.at[c, peer, pl.ds(0, SENT)],
            dst_ref=recv_q.at[c, slot, pl.ds(0, SENT)],
            send_sem=q_ss.at[c, peer],
            recv_sem=q_rs.at[c, slot],
            device_id={"seq": peer},
            device_id_type=MESH,
        )

    def xkv_copy(peer, slot):
        return pltpu.make_async_remote_copy(
            src_ref=xkv_send.at[peer],
            dst_ref=xkv_recv.at[slot],
            send_sem=xkv_ss.at[peer],
            recv_sem=xkv_rs.at[slot],
            device_id={"seq": peer},
            device_id_type=MESH,
        )

    def xq_copy(c, peer, slot):
        return pltpu.make_async_remote_copy(
            src_ref=xq_send.at[c, peer],
            dst_ref=xq_recv.at[c, slot],
            send_sem=xq_ss.at[c, peer],
            recv_sem=xq_rs.at[c, slot],
            device_id={"seq": peer},
            device_id_type=MESH,
        )

    def kv_copies(peer, slot):
        return [kv_copy(peer, slot)] + ([xkv_copy(peer, slot)] if TRIM else [])

    def q_copies(c, peer, slot):
        return [q_copy(c, peer, slot)] + ([xq_copy(c, peer, slot)] if TRIM else [])

    def start(copies):
        for copy in copies:
            copy.start()

    def wait_recv(copies):
        for copy in copies:
            copy.wait_recv()

    def wait_send(copies):
        for copy in copies:
            copy.wait_send()

    def put_last(row, block):
        first_row = iota((16, row.shape[-1]), 0) == 0
        block[...] = jnp.where(first_row, row, 0.0).astype(BF16)

    def each_peer(fn):
        def step(j, _):
            fn(peer_of(j))
            return 0

        lax.fori_loop(1, D, step, 0)

    def fill_q(c):
        rows = dot_nn(packed_v[...], wq_v[c]).astype(BF16)
        send_q[c] = rows.reshape(D, S, CHUNK)
        if TRIM:
            for p in range(D):
                xq_send[c, p] = rows[p * S + SENT : p * S + SENT + 1].astype(F32)

    def keep_q(c):
        recv_q[c, me] = send_q[c, me]
        if TRIM:
            xq_recv[c, me] = xq_send[c, me]

    def project(c, _):
        q_load(c).wait()
        fill_q(c)
        keep_q(c)

        @pl.when(c == 1)
        def _():
            each_peer(lambda p: start(q_copies(c, p, me)))

        return 0

    q_load(0).wait()
    for c in range(1, NC):
        q_load(c).start()
    grad_load.start()
    fill_q(0)
    pl.semaphore_wait(barrier, D - 1 + BITS)
    each_peer(lambda p: start(q_copies(0, p, me)))
    keep_q(0)

    place = hot * (dest - dev * R + 1).astype(F32)
    mine = jnp.where(me * S + within == iota((SLOTS, R), 0), 1.0, 0.0)
    places = dot_nt(place.astype(BF16), mine.astype(BF16))
    len_load.wait()
    rotation = (WINDOW // 2 - D // 2 * R) % PAIR_POSITIONS
    total = PC * PAIR_POSITIONS
    first = lax.rem(me * R - WINDOW + rotation + total, total)
    pair_a = first // PAIR_POSITIONS
    pair_b = lax.rem(pair_a + 1, PC)
    len_a = len_ref[pair_a]
    len_b = len_ref[pair_b]

    def segment_of(position):
        u = position + rotation
        u = jnp.where(u >= total, u - total, u)
        pair = lax.shift_right_arithmetic(u, jnp.full_like(u, log2(PAIR_POSITIONS)))
        within = u - pair * PAIR_POSITIONS
        limit = jnp.where(pair == pair_a, len_a, len_b)
        return 2 * pair + jnp.where(within >= limit, 1, 0)

    logp_load.wait()
    row_seg = segment_of(me * R + iota((1, R), 1))
    spread = jnp.where(row_seg == iota((LANES, R), 0), logp_v[...], 0.0)
    local_tot = jnp.sum(spread.T, axis=0, keepdims=True)
    for p in range(D):
        note_send[p, :, 0:SLOTS] = places[p : p + 1, :]
        note_send[p, :, SLOTS:] = local_tot
    each_peer(lambda p: note_copy(p, me).start())
    note_recv[me] = note_send[me]

    wkv_load.wait()
    UNI = FEAT // 10

    def untangle(b, _):
        rows = pl.multiple_of(b * UNI, 16)
        wkv_f[...] = wkv_raw[pl.ds(pl.multiple_of(b * UNI * KH, 16), UNI * KH), :].astype(F32)
        for h in range(KH):
            wkv_v[pl.ds(rows, UNI), h * 2 * HD : (h + 1) * 2 * HD] = wkv_f[
                pl.ds(h, UNI, stride=KH), :
            ].astype(BF16)
        return 0

    lax.fori_loop(0, FEAT // UNI, untangle, 0)
    kv_rows = dot_nn(packed_v[...], wkv_v[...]).astype(BF16)
    send_kv[...] = kv_rows.reshape(D, S, KC)
    if TRIM:
        for p in range(D):
            xkv_send[p] = kv_rows[p * S + SENT : p * S + SENT + 1].astype(F32)
    each_peer(lambda p: start(kv_copies(p, me)))
    recv_kv[me] = send_kv[me]
    if TRIM:
        xkv_recv[me] = xkv_send[me]

    lax.fori_loop(1, NC, project, 0)

    for r in range(R // WINDOW):
        base = me * R + r * WINDOW
        key_pos = base - WINDOW + iota((2 * WINDOW, 1), 0)
        query_pos = base + iota((1, WINDOW), 1)
        offset = query_pos - key_pos
        key_seg = segment_of(key_pos)
        query_seg = segment_of(query_pos)
        allowed = (
            (key_pos >= 0) & (offset >= 0) & (offset < WINDOW) & (key_seg == query_seg)
        )
        bias_v[r] = jnp.where(allowed, 0.0, NEG_FILL)

    each_peer(lambda p: note_copy(p, p).wait_recv())
    notes = jnp.sum(note_recv[...], axis=0)
    place_v[...] = jnp.where(
        iota((R, SLOTS), 0) + 1 == notes[:, 0:SLOTS].astype(jnp.int32), 1.0, 0.0
    ).astype(BF16)[:, 0 : D * S]
    seg_tot = notes[:, SLOTS:]
    lane = iota((1, LANES), 1)
    seg_len = jnp.ones((1, LANES), jnp.int32)
    for p in range(PC):
        seg_len = jnp.where(lane == 2 * p, len_ref[p], seg_len)
        seg_len = jnp.where(lane == 2 * p + 1, PAIR_POSITIONS - len_ref[p], seg_len)
    seg_len = seg_len.astype(F32)
    mean = seg_tot / seg_len
    margin = BETA * (mean - pltpu.roll(mean, LANES - 1, 1)) - GAMMA
    neg = -margin
    tail = jnp.exp(-jnp.abs(neg))
    loss = jnp.maximum(neg, 0.0) + jnp.log1p(tail)
    for p in range(PC):
        loss_ref[p] = jnp.sum(jnp.where(lane == 2 * p, loss, 0.0))
    loss_store.start()
    weight = jnp.where(neg >= 0, 1.0 / (1.0 + tail), tail / (1.0 + tail)) * (BETA * LOSS_SCALE)
    even = (lane & 1) == 0
    coef = jnp.where(even, -weight, pltpu.roll(weight, 1, 1)) / seg_len
    col_seg = segment_of(me * R + iota((R, 1), 0))
    coef_v[...] = jnp.broadcast_to(
        jnp.sum(jnp.where(col_seg == iota((R, LANES), 1), coef, 0.0), axis=1, keepdims=True),
        (R, LANES),
    )

    dk4[...] = jnp.zeros_like(dk4)
    dv4[...] = jnp.zeros_like(dv4)

    each_peer(lambda p: wait_recv(kv_copies(p, p)))
    if NC > 2:
        each_peer(lambda p: start(q_copies(2, p, me)))
    if TRIM:
        for p in range(D):
            put_last(xkv_recv[p], recv_kv.at[p, SENT : SENT + 16])
    kvx[WINDOW:] = dot_nn(place_v[...], recv_kv[...].reshape(D * S, KC)).astype(BF16)

    edge = pltpu.make_async_remote_copy(
        src_ref=kvx.at[pl.ds(R, WINDOW)],
        dst_ref=kvx.at[pl.ds(0, WINDOW)],
        send_sem=edge_ss,
        recv_sem=edge_rs,
        device_id={"seq": lax.rem(me + 1, D)},
        device_id_type=MESH,
    )

    @pl.when(me < D - 1)
    def _():
        edge.start()

    grad_load.wait()

    @pl.when(me > 0)
    def _():
        edge.wait_recv()

    low = iota((R + WINDOW, LANES), 1) < HD
    for h in range(KH):
        kv = kvx[:, h * 2 * HD : (h + 1) * 2 * HD].astype(F32)
        turned = pltpu.roll(kv, HD, 1)
        kk = jnp.where(low, kv, turned).astype(BF16)
        vv = jnp.where(low, turned, kv).astype(BF16)
        for g in range(CHUNK // LANES):
            k4[h, :, g * LANES : (g + 1) * LANES] = kk
            v4[h, :, g * LANES : (g + 1) * LANES] = vv

    head_of = lax.shift_right_arithmetic(
        iota((WINDOW, CHUNK), 1), jnp.full((WINDOW, CHUNK), log2(HD), jnp.int32)
    )

    def spread_heads(x):
        return jnp.concatenate(
            [jnp.where(head_of == g, x, 0.0).astype(BF16) for g in range(HPC)], axis=0
        )

    halo = pltpu.make_async_remote_copy(
        src_ref=halo_send,
        dst_ref=halo_recv,
        send_sem=halo_ss,
        recv_sem=halo_rs,
        device_id={"seq": lax.rem(me + D - 1, D)},
        device_id_type=MESH,
    )

    def fold(h, rows):
        folded = []
        for acc in (dk4, dv4):
            y = acc[h, rows, 0:LANES]
            for g in range(1, CHUNK // LANES):
                y = y + acc[h, rows, g * LANES : (g + 1) * LANES]
            folded.append(y + pltpu.roll(y, HD, 1))
        return jnp.where(low[rows], folded[0] * scale, folded[1])

    def attend(c, _):
        h = c // CPK
        each_peer(lambda p: wait_recv(q_copies(c, p, p)))

        @pl.when(c + 3 < NC)
        def _():
            each_peer(lambda p: start(q_copies(c + 3, p, me)))

        if TRIM:
            for p in range(D):
                put_last(xq_recv[c, p], recv_q.at[c, p, SENT : SENT + 16])
        q_all = dot_nn(place_v[...], recv_q[c].reshape(D * S, CHUNK))
        g_all = grad_v[:, pl.ds(pl.multiple_of(c * CHUNK, CHUNK), CHUNK)].astype(F32)
        factor = coef_v[...]
        g_all = g_all * jnp.concatenate([factor] * (CHUNK // LANES), axis=1)
        sink = jnp.concatenate(
            [jnp.full((1, WINDOW), sink_ref[c * HPC + g], F32) for g in range(HPC)], axis=1
        )
        for r in range(R // WINDOW):
            rows = slice(r * WINDOW, (r + 1) * WINDOW)
            keys = slice(r * WINDOW, (r + 2) * WINDOW)
            qz = spread_heads(q_all[rows])
            gz = spread_heads(g_all[rows])
            kr = k4[h, keys, :]
            vr = v4[h, keys, :]
            bias = bias_v[r]
            masked = dot_nt(kr, qz) * scale + jnp.concatenate([bias] * HPC, axis=1)
            top = jnp.maximum(jnp.max(masked, axis=0, keepdims=True), sink)
            expo = jnp.exp(masked - top)
            denom = jnp.exp(sink - top) + jnp.sum(expo, axis=0, keepdims=True)
            probs = expo * (1.0 / denom)
            probs_b = probs.astype(BF16)
            prob_grad = dot_nt(vr, gz)
            row_dot = jnp.sum(probs_b.astype(F32) * prob_grad, axis=0, keepdims=True)
            score_grad = (probs * (prob_grad - row_dot)).astype(BF16)
            dk4[h, keys, :] += dot_nn(score_grad, qz)
            dv4[h, keys, :] += dot_nn(probs_b, gz)
            if r == 0:

                @pl.when(c == NC - 1)
                def _():
                    for k in range(KH):
                        halo_send[:, k * 2 * HD : (k + 1) * 2 * HD] = fold(
                            k, slice(0, WINDOW)
                        ).astype(BF16)

                @pl.when((c == NC - 1) & (me > 0))
                def _():
                    halo.start()

            wide = dot_tn(score_grad, kr)
            dq = jnp.where(head_of == 0, wide[0:WINDOW], 0.0)
            for g in range(1, HPC):
                dq = jnp.where(head_of == g, wide[g * WINDOW : (g + 1) * WINDOW], dq)
            dq_v[c, rows, :] = (dq * scale).astype(BF16)
        return 0

    sink_load.wait()
    lax.fori_loop(0, NC, attend, 0)

    for h in range(KH):
        cols = slice(h * 2 * HD, (h + 1) * 2 * HD)
        kvg_f[:, cols] = fold(h, slice(WINDOW, WINDOW + R))

    def ranges(s, n):
        off, size = bounds[n]
        order = list(range(BITS)) if n % 2 == 0 else list(reversed(range(BITS)))
        for t in range(s + 1):
            size //= 2
            bit = bit_of(order[t])
            keep = off + bit * size
            give = off + (1 - bit) * size
            off = keep
        return pl.multiple_of(keep, 16), pl.multiple_of(give, 16), size, partner_of(order[s])

    def landing(s, n):
        o, w = bounds[n]
        size = w >> (s + 1)
        return pl.ds(o + w - 2 * size, size)

    def rs_copy(s, n):
        keep, give, size, partner = ranges(s, n)
        return pltpu.make_async_remote_copy(
            src_ref=part.at[pl.ds(give, size)],
            dst_ref=rs_recv.at[landing(s, n)],
            send_sem=rs_ss.at[s, n],
            recv_sem=rs_rs.at[s, n],
            device_id={"head": partner},
            device_id_type=MESH,
        )

    def ag_copy(s, n, mine):
        keep, give, size, partner = ranges(s, n)
        rows = pl.ds(keep if mine else give, size)
        return pltpu.make_async_remote_copy(
            src_ref=(part if s == BITS - 1 else out_ref).at[rows],
            dst_ref=out_ref.at[rows],
            send_sem=ag_ss.at[s, n],
            recv_sem=ag_rs.at[s, n],
            device_id={"head": partner},
            device_id_type=MESH,
        )

    def own_copy(n):
        keep, give, size, partner = ranges(BITS - 1, n)
        rows = pl.ds(keep, size)
        return pltpu.make_async_copy(part.at[rows], out_ref.at[rows], own_sem.at[n])

    def query_part(n):
        o, w = bounds[n]
        e = min(o + w, FEAT)
        acc = dot_nt(wq_v[0, o:e, :], dq_v[0])
        for c in range(1, NC):
            acc = acc + dot_nt(wq_v[c, o:e, :], dq_v[c])
        return acc

    early = [query_part(n) for n in range(AHEAD)]

    @pl.when(me < D - 1)
    def _():
        halo.wait_recv()

    kvg_b[0 : R - WINDOW] = kvg_f[0 : R - WINDOW].astype(BF16)
    kvg_b[R - WINDOW :] = (kvg_f[R - WINDOW :] + halo_recv[...].astype(F32)).astype(BF16)
    for n, (o, w) in enumerate(bounds):
        e = min(o + w, FEAT)
        acc = early[n] if n < AHEAD else query_part(n)
        acc = acc + dot_nt(wkv_v[o:e, :], kvg_b[...])
        part[o:e, :] = acc.astype(BF16)
        if o + w > e:
            part[e : o + w, :] = jnp.zeros((o + w - e, R), BF16)
        rs_copy(0, n).start()

    for s in range(BITS):
        for n in range(len(bounds)):
            rs_copy(s, n).wait_recv()
            keep, give, size, partner = ranges(s, n)
            added = part[pl.ds(keep, size), :].astype(F32) + rs_recv[landing(s, n), :].astype(F32)
            part[pl.ds(keep, size), :] = added.astype(BF16)
            if s < BITS - 1:
                rs_copy(s + 1, n).start()
            else:
                ag_copy(s, n, True).start()
                own_copy(n).start()

    for s in reversed(range(BITS)):
        for n in range(len(bounds)):
            ag_copy(s, n, False).wait_recv()
            if s == BITS - 1:
                own_copy(n).wait()
            if s > 0:
                ag_copy(s - 1, n, True).start()

    each_peer(lambda p: note_copy(p, me).wait_send())
    each_peer(lambda p: wait_send(kv_copies(p, me)))
    for c in range(NC):
        each_peer(lambda p: wait_send(q_copies(c, p, me)))

    @pl.when(me < D - 1)
    def _():
        edge.wait_send()

    @pl.when(me > 0)
    def _():
        halo.wait_send()

    for s in range(BITS):
        for n in range(len(bounds)):
            rs_copy(s, n).wait_send()
            ag_copy(s, n, True).wait_send()
    loss_store.wait()


def local(hidden, dest_pos, chosen_len, token_logp, head_grad, q_weight, key_value_weight, sinks):
    D, N = lax.axis_size("seq"), lax.axis_size("head")
    R, FEAT = hidden.shape
    HD = key_value_weight.shape[2] // 2
    KH = key_value_weight.shape[1]
    KC = KH * 2 * HD
    QC = q_weight.shape[1]
    PC = chosen_len.shape[0]
    S = -(-(R // D + 1) // 16) * 16
    NC = QC // CHUNK
    BITS = log2(N)
    SLOTS = -(-(D * S) // LANES) * LANES
    bounds = chunk_bounds(FEAT, N)
    NB = len(bounds)
    wide = bounds[-1][0] + bounds[-1][1]
    cfg = (D, N, R, S, QC, KC, FEAT, HD, PC)
    hbm = pl.BlockSpec(memory_space=pltpu.HBM)
    anywhere = pl.BlockSpec(memory_space=pl.ANY)
    dma = pltpu.SemaphoreType.DMA
    grad, loss = pl.pallas_call(
        functools.partial(kernel, cfg),
        out_shape=(
            pltpu.VMEM((wide, R), BF16),
            jax.ShapeDtypeStruct((PC,), F32),
        ),
        in_specs=[hbm] * 8,
        out_specs=(anywhere, hbm),
        scratch_shapes=[
            pltpu.SMEM((PC,), jnp.int32),
            pltpu.SMEM(sinks.shape, F32),
            pltpu.SMEM((PC,), F32),
            pltpu.VMEM((1, R), jnp.int32),
            pltpu.VMEM((1, R), F32),
            pltpu.VMEM((FEAT, R), BF16),
            pltpu.VMEM((R, QC), BF16),
            pltpu.VMEM((NC, FEAT, CHUNK), BF16),
            pltpu.VMEM((FEAT * KH, 2 * HD), BF16),
            pltpu.VMEM((FEAT // 10 * KH, 2 * HD), F32),
            pltpu.VMEM((FEAT, KC), BF16),
            pltpu.VMEM((D * S, FEAT), BF16),
            pltpu.VMEM((D, S, KC), BF16),
            pltpu.VMEM((D, S, KC), BF16),
            pltpu.VMEM((NC, D, S, CHUNK), BF16),
            pltpu.VMEM((NC, D, S, CHUNK), BF16),
            pltpu.VMEM((D, 1, SLOTS + LANES), F32),
            pltpu.VMEM((D, 1, SLOTS + LANES), F32),
            pltpu.VMEM((D, 1, KC), F32),
            pltpu.VMEM((D, 1, KC), F32),
            pltpu.VMEM((NC, D, 1, CHUNK), F32),
            pltpu.VMEM((NC, D, 1, CHUNK), F32),
            pltpu.VMEM((R, D * S), BF16),
            pltpu.VMEM((R + WINDOW, KC), BF16),
            pltpu.VMEM((KH, R + WINDOW, CHUNK), BF16),
            pltpu.VMEM((KH, R + WINDOW, CHUNK), BF16),
            pltpu.VMEM((R // WINDOW, 2 * WINDOW, WINDOW), F32),
            pltpu.VMEM((R, LANES), F32),
            pltpu.VMEM((KH, R + WINDOW, CHUNK), F32),
            pltpu.VMEM((KH, R + WINDOW, CHUNK), F32),
            pltpu.VMEM((NC, R, CHUNK), BF16),
            pltpu.VMEM((R, KC), BF16),
            pltpu.VMEM((R, KC), F32),
            pltpu.VMEM((WINDOW, KC), BF16),
            pltpu.VMEM((WINDOW, KC), BF16),
            pltpu.VMEM((wide, R), BF16),
            pltpu.VMEM((wide, R), BF16),
            dma((5 + NC,)),
            dma((D,)),
            dma((D,)),
            dma((NC, D)),
            dma((NC, D)),
            dma((D,)),
            dma((D,)),
            dma,
            dma,
            dma,
            dma,
            dma((BITS, NB)),
            dma((BITS, NB)),
            dma((BITS, NB)),
            dma((BITS, NB)),
            dma((NB,)),
            dma((3,)),
            dma((D,)),
            dma((D,)),
            dma((NC, D)),
            dma((NC, D)),
        ],
        compiler_params=pltpu.CompilerParams(
            collective_id=0, has_side_effects=True, vmem_limit_bytes=60 * 1024 * 1024
        ),
        name="preference_gradient",
    )(
        chosen_len,
        sinks,
        dest_pos.reshape(1, R),
        token_logp.reshape(1, R),
        hidden.T,
        head_grad,
        q_weight,
        key_value_weight.reshape(FEAT * KH, 2 * HD),
    )
    return grad[:FEAT].T, loss


def solution(mesh):
    placed = (
        P(("batch", "seq"), None),
        P(("batch", "seq")),
        P("batch"),
        P(("batch", "seq")),
        P(("batch", "seq"), "head"),
        P(None, "head"),
        P(None, "head", None),
        P("head"),
    )
    return jax.shard_map(
        local,
        mesh=mesh,
        in_specs=placed,
        out_specs=(P(("batch", "seq"), None), P("batch")),
        check_vma=False,
    )
```

```python
import functools

import jax
import jax.numpy as jnp
from jax import lax
from jax.experimental import pallas as pl
from jax.experimental.pallas import tpu as pltpu
from jax.sharding import PartitionSpec as P

WINDOW = 128
PAIR_POSITIONS = 512
BETA = 2.0
GAMMA = 1.0
LOSS_SCALE = 256.0
NEG_FILL = -1e30
LANES = 128
CHUNK = 256
OUT_CHUNKS = 6
AHEAD = 3
F32 = jnp.float32
BF16 = jnp.bfloat16
MESH = pl.DeviceIdType.MESH


def dot_nn(a, b):
    return lax.dot_general(a, b, (((1,), (0,)), ((), ())), preferred_element_type=F32)


def dot_nt(a, b):
    return lax.dot_general(a, b, (((1,), (1,)), ((), ())), preferred_element_type=F32)


def dot_tn(a, b):
    return lax.dot_general(a, b, (((0,), (0,)), ((), ())), preferred_element_type=F32)


def iota(shape, dim):
    return lax.broadcasted_iota(jnp.int32, shape, dim)


def log2(n):
    assert n & (n - 1) == 0
    return n.bit_length() - 1


def chunk_bounds(feat, n):
    unit = 16 * n
    units = -(-feat // unit)
    count = min(OUT_CHUNKS, units)
    sizes = [unit * ((units + k) // count) for k in range(count)]
    return [(sum(sizes[:k]), sizes[k]) for k in range(count)]


def kernel(
    cfg,
    len_hbm,
    sink_hbm,
    dest_hbm,
    logp_hbm,
    hidden_hbm,
    grad_hbm,
    wq_hbm,
    wkv_hbm,
    out_ref,
    loss_hbm,
    len_ref,
    sink_ref,
    loss_ref,
    dest_v,
    logp_v,
    hidden_v,
    grad_v,
    wq_v,
    wkv_raw,
    wkv_f,
    wkv_v,
    packed_v,
    send_kv,
    recv_kv,
    send_q,
    recv_q,
    note_send,
    note_recv,
    xkv_send,
    xkv_recv,
    xq_send,
    xq_recv,
    place_v,
    kvx,
    k4,
    v4,
    bias_v,
    coef_v,
    dk4,
    dv4,
    dq_v,
    kvg_b,
    kvg_f,
    halo_send,
    halo_recv,
    part,
    rs_recv,
    load_sem,
    kv_ss,
    kv_rs,
    q_ss,
    q_rs,
    note_ss,
    note_rs,
    edge_ss,
    edge_rs,
    halo_ss,
    halo_rs,
    rs_ss,
    rs_rs,
    ag_ss,
    ag_rs,
    own_sem,
    small_sem,
    xkv_ss,
    xkv_rs,
    xq_ss,
    xq_rs,
):
    D, N, R, S, QC, KC, FEAT, HD, PC = cfg
    TRIM = R // D % 16 == 0
    SENT = R // D if TRIM else -(-(R // D + 1) // 8) * 8
    NC = QC // CHUNK
    KH = KC // (2 * HD)
    HPC = CHUNK // HD
    CPK = NC // KH
    BITS = log2(N)
    SLOTS = -(-(D * S) // LANES) * LANES
    scale = HD ** (-0.5)
    me = lax.axis_index("seq")
    hd = lax.axis_index("head")
    bounds = chunk_bounds(FEAT, N)

    loads = [
        pltpu.make_async_copy(dest_hbm, dest_v, load_sem.at[0]),
        pltpu.make_async_copy(hidden_hbm, hidden_v, load_sem.at[1]),
    ]

    def q_load(c):
        columns = pl.ds(pl.multiple_of(c * CHUNK, CHUNK), CHUNK)
        return pltpu.make_async_copy(wq_hbm.at[:, columns], wq_v.at[c], load_sem.at[5 + c])

    logp_load = pltpu.make_async_copy(logp_hbm, logp_v, load_sem.at[2])
    wkv_load = pltpu.make_async_copy(wkv_hbm, wkv_raw, load_sem.at[3])
    grad_load = pltpu.make_async_copy(grad_hbm, grad_v, load_sem.at[4])
    len_load = pltpu.make_async_copy(len_hbm, len_ref, small_sem.at[0])
    sink_load = pltpu.make_async_copy(sink_hbm, sink_ref, small_sem.at[1])
    loss_store = pltpu.make_async_copy(loss_ref, loss_hbm, small_sem.at[2])
    for load in loads:
        load.start()
    q_load(0).start()
    len_load.start()
    sink_load.start()

    halo_recv[...] = jnp.zeros_like(halo_recv)
    kvx[0:WINDOW] = jnp.zeros((WINDOW, KC), BF16)
    recv_kv[:, S - 16 :, :] = jnp.zeros((D, 16, KC), BF16)
    recv_q[:, :, S - 16 :, :] = jnp.zeros((NC, D, 16, CHUNK), BF16)

    def peer_of(j):
        return lax.rem(me + j, D)

    def bit_of(b):
        return lax.rem(hd // (1 << b), 2)

    def partner_of(b):
        return hd + (1 - 2 * bit_of(b)) * (1 << b)

    barrier = pltpu.get_barrier_semaphore()

    def greet(j, _):
        pl.semaphore_signal(
            barrier, inc=1, device_id={"seq": peer_of(j)}, device_id_type=MESH
        )
        return 0

    lax.fori_loop(1, D, greet, 0)
    for b in range(BITS):
        pl.semaphore_signal(
            barrier, inc=1, device_id={"head": partner_of(b)}, device_id_type=MESH
        )

    loads[0].wait()
    dest = dest_v[...]
    dev = lax.shift_right_arithmetic(dest, jnp.full_like(dest, log2(R)))
    DP = max(16, D)
    hot = jnp.where(dev == iota((DP, R), 0), 1.0, 0.0)
    upper = jnp.where(iota((R, R), 0) < iota((R, R), 1), 1.0, 0.0).astype(BF16)
    before = dot_nn(hot.astype(BF16), upper)
    within = jnp.sum(hot * before, axis=0, keepdims=True).astype(jnp.int32)
    pack = jnp.where(dev * S + within == iota((D * S, R), 0), 1.0, 0.0).astype(BF16)

    loads[1].wait()
    logp_load.start()
    wkv_load.start()
    for o in range(0, FEAT, 4 * LANES):
        w = min(4 * LANES, FEAT - o)
        packed_v[:, o : o + w] = dot_nt(pack, hidden_v[o : o + w, :]).astype(BF16)

    def note_copy(peer, slot):
        return pltpu.make_async_remote_copy(
            src_ref=note_send.at[peer],
            dst_ref=note_recv.at[slot],
            send_sem=note_ss.at[peer],
            recv_sem=note_rs.at[slot],
            device_id={"seq": peer},
            device_id_type=MESH,
        )

    def kv_copy(peer, slot):
        return pltpu.make_async_remote_copy(
            src_ref=send_kv.at[peer, pl.ds(0, SENT)],
            dst_ref=recv_kv.at[slot, pl.ds(0, SENT)],
            send_sem=kv_ss.at[peer],
            recv_sem=kv_rs.at[slot],
            device_id={"seq": peer},
            device_id_type=MESH,
        )

    def q_copy(c, peer, slot):
        return pltpu.make_async_remote_copy(
            src_ref=send_q.at[c, peer, pl.ds(0, SENT)],
            dst_ref=recv_q.at[c, slot, pl.ds(0, SENT)],
            send_sem=q_ss.at[c, peer],
            recv_sem=q_rs.at[c, slot],
            device_id={"seq": peer},
            device_id_type=MESH,
        )

    def xkv_copy(peer, slot):
        return pltpu.make_async_remote_copy(
            src_ref=xkv_send.at[peer],
            dst_ref=xkv_recv.at[slot],
            send_sem=xkv_ss.at[peer],
            recv_sem=xkv_rs.at[slot],
            device_id={"seq": peer},
            device_id_type=MESH,
        )

    def xq_copy(c, peer, slot):
        return pltpu.make_async_remote_copy(
            src_ref=xq_send.at[c, peer],
            dst_ref=xq_recv.at[c, slot],
            send_sem=xq_ss.at[c, peer],
            recv_sem=xq_rs.at[c, slot],
            device_id={"seq": peer},
            device_id_type=MESH,
        )

    def kv_copies(peer, slot):
        return [kv_copy(peer, slot)] + ([xkv_copy(peer, slot)] if TRIM else [])

    def q_copies(c, peer, slot):
        return [q_copy(c, peer, slot)] + ([xq_copy(c, peer, slot)] if TRIM else [])

    def start(copies):
        for copy in copies:
            copy.start()

    def wait_recv(copies):
        for copy in copies:
            copy.wait_recv()

    def wait_send(copies):
        for copy in copies:
            copy.wait_send()

    def put_last(row, block):
        first_row = iota((16, row.shape[-1]), 0) == 0
        block[...] = jnp.where(first_row, row, 0.0).astype(BF16)

    def each_peer(fn):
        def step(j, _):
            fn(peer_of(j))
            return 0

        lax.fori_loop(1, D, step, 0)

    def fill_q(c):
        rows = dot_nn(packed_v[...], wq_v[c]).astype(BF16)
        send_q[c] = rows.reshape(D, S, CHUNK)
        if TRIM:
            for p in range(D):
                xq_send[c, p] = rows[p * S + SENT : p * S + SENT + 1].astype(F32)

    def keep_q(c):
        recv_q[c, me] = send_q[c, me]
        if TRIM:
            xq_recv[c, me] = xq_send[c, me]

    def project(c, _):
        q_load(c).wait()
        fill_q(c)
        keep_q(c)

        @pl.when(c == 1)
        def _():
            each_peer(lambda p: start(q_copies(c, p, me)))

        return 0

    q_load(0).wait()
    for c in range(1, NC):
        q_load(c).start()
    grad_load.start()
    fill_q(0)
    pl.semaphore_wait(barrier, D - 1 + BITS)
    each_peer(lambda p: start(q_copies(0, p, me)))
    keep_q(0)

    place = hot * (dest - dev * R + 1).astype(F32)
    mine = jnp.where(me * S + within == iota((SLOTS, R), 0), 1.0, 0.0)
    places = dot_nt(place.astype(BF16), mine.astype(BF16))
    len_load.wait()
    rotation = (WINDOW // 2 - D // 2 * R) % PAIR_POSITIONS
    total = PC * PAIR_POSITIONS
    first = lax.rem(me * R - WINDOW + rotation + total, total)
    pair_a = first // PAIR_POSITIONS
    pair_b = lax.rem(pair_a + 1, PC)
    len_a = len_ref[pair_a]
    len_b = len_ref[pair_b]

    def segment_of(position):
        u = position + rotation
        u = jnp.where(u >= total, u - total, u)
        pair = lax.shift_right_arithmetic(u, jnp.full_like(u, log2(PAIR_POSITIONS)))
        within = u - pair * PAIR_POSITIONS
        limit = jnp.where(pair == pair_a, len_a, len_b)
        return 2 * pair + jnp.where(within >= limit, 1, 0)

    logp_load.wait()
    row_seg = segment_of(me * R + iota((1, R), 1))
    spread = jnp.where(row_seg == iota((LANES, R), 0), logp_v[...], 0.0)
    local_tot = jnp.sum(spread.T, axis=0, keepdims=True)
    for p in range(D):
        note_send[p, :, 0:SLOTS] = places[p : p + 1, :]
        note_send[p, :, SLOTS:] = local_tot
    each_peer(lambda p: note_copy(p, me).start())
    note_recv[me] = note_send[me]

    wkv_load.wait()
    UNI = FEAT // 10

    def untangle(b, _):
        rows = pl.multiple_of(b * UNI, 16)
        wkv_f[...] = wkv_raw[pl.ds(pl.multiple_of(b * UNI * KH, 16), UNI * KH), :].astype(F32)
        for h in range(KH):
            wkv_v[pl.ds(rows, UNI), h * 2 * HD : (h + 1) * 2 * HD] = wkv_f[
                pl.ds(h, UNI, stride=KH), :
            ].astype(BF16)
        return 0

    lax.fori_loop(0, FEAT // UNI, untangle, 0)
    kv_rows = dot_nn(packed_v[...], wkv_v[...]).astype(BF16)
    send_kv[...] = kv_rows.reshape(D, S, KC)
    if TRIM:
        for p in range(D):
            xkv_send[p] = kv_rows[p * S + SENT : p * S + SENT + 1].astype(F32)
    each_peer(lambda p: start(kv_copies(p, me)))
    recv_kv[me] = send_kv[me]
    if TRIM:
        xkv_recv[me] = xkv_send[me]

    lax.fori_loop(1, NC, project, 0)

    for r in range(R // WINDOW):
        base = me * R + r * WINDOW
        key_pos = base - WINDOW + iota((2 * WINDOW, 1), 0)
        query_pos = base + iota((1, WINDOW), 1)
        offset = query_pos - key_pos
        key_seg = segment_of(key_pos)
        query_seg = segment_of(query_pos)
        allowed = (
            (key_pos >= 0) & (offset >= 0) & (offset < WINDOW) & (key_seg == query_seg)
        )
        bias_v[r] = jnp.where(allowed, 0.0, NEG_FILL)

    each_peer(lambda p: note_copy(p, p).wait_recv())
    notes = jnp.sum(note_recv[...], axis=0)
    place_v[...] = jnp.where(
        iota((R, SLOTS), 0) + 1 == notes[:, 0:SLOTS].astype(jnp.int32), 1.0, 0.0
    ).astype(BF16)[:, 0 : D * S]
    seg_tot = notes[:, SLOTS:]
    lane = iota((1, LANES), 1)
    seg_len = jnp.ones((1, LANES), jnp.int32)
    for p in range(PC):
        seg_len = jnp.where(lane == 2 * p, len_ref[p], seg_len)
        seg_len = jnp.where(lane == 2 * p + 1, PAIR_POSITIONS - len_ref[p], seg_len)
    seg_len = seg_len.astype(F32)
    mean = seg_tot / seg_len
    margin = BETA * (mean - pltpu.roll(mean, LANES - 1, 1)) - GAMMA
    neg = -margin
    tail = jnp.exp(-jnp.abs(neg))
    loss = jnp.maximum(neg, 0.0) + jnp.log1p(tail)
    for p in range(PC):
        loss_ref[p] = jnp.sum(jnp.where(lane == 2 * p, loss, 0.0))
    loss_store.start()
    weight = jnp.where(neg >= 0, 1.0 / (1.0 + tail), tail / (1.0 + tail)) * (BETA * LOSS_SCALE)
    even = (lane & 1) == 0
    coef = jnp.where(even, -weight, pltpu.roll(weight, 1, 1)) / seg_len
    col_seg = segment_of(me * R + iota((R, 1), 0))
    coef_v[...] = jnp.broadcast_to(
        jnp.sum(jnp.where(col_seg == iota((R, LANES), 1), coef, 0.0), axis=1, keepdims=True),
        (R, LANES),
    )

    dk4[...] = jnp.zeros_like(dk4)
    dv4[...] = jnp.zeros_like(dv4)

    each_peer(lambda p: wait_recv(kv_copies(p, p)))
    if NC > 2:
        each_peer(lambda p: start(q_copies(2, p, me)))
    if TRIM:
        for p in range(D):
            put_last(xkv_recv[p], recv_kv.at[p, SENT : SENT + 16])
    kvx[WINDOW:] = dot_nn(place_v[...], recv_kv[...].reshape(D * S, KC)).astype(BF16)

    edge = pltpu.make_async_remote_copy(
        src_ref=kvx.at[pl.ds(R, WINDOW)],
        dst_ref=kvx.at[pl.ds(0, WINDOW)],
        send_sem=edge_ss,
        recv_sem=edge_rs,
        device_id={"seq": lax.rem(me + 1, D)},
        device_id_type=MESH,
    )

    @pl.when(me < D - 1)
    def _():
        edge.start()

    grad_load.wait()

    @pl.when(me > 0)
    def _():
        edge.wait_recv()

    low = iota((R + WINDOW, LANES), 1) < HD
    for h in range(KH):
        kv = kvx[:, h * 2 * HD : (h + 1) * 2 * HD].astype(F32)
        turned = pltpu.roll(kv, HD, 1)
        kk = jnp.where(low, kv, turned).astype(BF16)
        vv = jnp.where(low, turned, kv).astype(BF16)
        for g in range(CHUNK // LANES):
            k4[h, :, g * LANES : (g + 1) * LANES] = kk
            v4[h, :, g * LANES : (g + 1) * LANES] = vv

    head_of = lax.shift_right_arithmetic(
        iota((WINDOW, CHUNK), 1), jnp.full((WINDOW, CHUNK), log2(HD), jnp.int32)
    )

    def spread_heads(x):
        return jnp.concatenate(
            [jnp.where(head_of == g, x, 0.0).astype(BF16) for g in range(HPC)], axis=0
        )

    halo = pltpu.make_async_remote_copy(
        src_ref=halo_send,
        dst_ref=halo_recv,
        send_sem=halo_ss,
        recv_sem=halo_rs,
        device_id={"seq": lax.rem(me + D - 1, D)},
        device_id_type=MESH,
    )

    def fold(h, rows):
        folded = []
        for acc in (dk4, dv4):
            y = acc[h, rows, 0:LANES]
            for g in range(1, CHUNK // LANES):
                y = y + acc[h, rows, g * LANES : (g + 1) * LANES]
            folded.append(y + pltpu.roll(y, HD, 1))
        return jnp.where(low[rows], folded[0] * scale, folded[1])

    def attend(c, _):
        h = c // CPK
        each_peer(lambda p: wait_recv(q_copies(c, p, p)))

        @pl.when(c + 3 < NC)
        def _():
            each_peer(lambda p: start(q_copies(c + 3, p, me)))

        if TRIM:
            for p in range(D):
                put_last(xq_recv[c, p], recv_q.at[c, p, SENT : SENT + 16])
        q_all = dot_nn(place_v[...], recv_q[c].reshape(D * S, CHUNK))
        g_all = grad_v[:, pl.ds(c * CHUNK if isinstance(c, int) else pl.multiple_of(c * CHUNK, CHUNK), CHUNK)].astype(F32)
        factor = coef_v[...]
        g_all = g_all * jnp.concatenate([factor] * (CHUNK // LANES), axis=1)
        sink = jnp.concatenate(
            [jnp.full((1, WINDOW), sink_ref[c * HPC + g], F32) for g in range(HPC)], axis=1
        )
        for r in range(R // WINDOW):
            rows = slice(r * WINDOW, (r + 1) * WINDOW)
            keys = slice(r * WINDOW, (r + 2) * WINDOW)
            qz = spread_heads(q_all[rows])
            gz = spread_heads(g_all[rows])
            kr = k4[h, keys, :]
            vr = v4[h, keys, :]
            bias = bias_v[r]
            masked = dot_nt(kr, qz) * scale + jnp.concatenate([bias] * HPC, axis=1)
            top = jnp.maximum(jnp.max(masked, axis=0, keepdims=True), sink)
            expo = jnp.exp(masked - top)
            denom = jnp.exp(sink - top) + jnp.sum(expo, axis=0, keepdims=True)
            probs = expo * (1.0 / denom)
            probs_b = probs.astype(BF16)
            prob_grad = dot_nt(vr, gz)
            row_dot = jnp.sum(probs_b.astype(F32) * prob_grad, axis=0, keepdims=True)
            score_grad = (probs * (prob_grad - row_dot)).astype(BF16)
            dk4[h, keys, :] += dot_nn(score_grad, qz)
            dv4[h, keys, :] += dot_nn(probs_b, gz)
            if r == 0 and isinstance(c, int):
                for k in range(KH):
                    halo_send[:, k * 2 * HD : (k + 1) * 2 * HD] = fold(
                        k, slice(0, WINDOW)
                    ).astype(BF16)

                @pl.when(me > 0)
                def _():
                    halo.start()

            wide = dot_tn(score_grad, kr)
            dq = jnp.where(head_of == 0, wide[0:WINDOW], 0.0)
            for g in range(1, HPC):
                dq = jnp.where(head_of == g, wide[g * WINDOW : (g + 1) * WINDOW], dq)
            dq_v[c, rows, :] = (dq * scale).astype(BF16)
        return 0

    sink_load.wait()
    lax.fori_loop(0, NC - 1, attend, 0)
    attend(NC - 1, 0)

    for h in range(KH):
        cols = slice(h * 2 * HD, (h + 1) * 2 * HD)
        kvg_f[:, cols] = fold(h, slice(WINDOW, WINDOW + R))

    def ranges(s, n):
        off, size = bounds[n]
        order = list(range(BITS)) if n % 2 == 0 else list(reversed(range(BITS)))
        for t in range(s + 1):
            size //= 2
            bit = bit_of(order[t])
            keep = off + bit * size
            give = off + (1 - bit) * size
            off = keep
        return pl.multiple_of(keep, 16), pl.multiple_of(give, 16), size, partner_of(order[s])

    def landing(s, n):
        o, w = bounds[n]
        size = w >> (s + 1)
        return pl.ds(o + w - 2 * size, size)

    def rs_copy(s, n):
        keep, give, size, partner = ranges(s, n)
        return pltpu.make_async_remote_copy(
            src_ref=part.at[pl.ds(give, size)],
            dst_ref=rs_recv.at[landing(s, n)],
            send_sem=rs_ss.at[s, n],
            recv_sem=rs_rs.at[s, n],
            device_id={"head": partner},
            device_id_type=MESH,
        )

    def ag_copy(s, n, mine):
        keep, give, size, partner = ranges(s, n)
        rows = pl.ds(keep if mine else give, size)
        return pltpu.make_async_remote_copy(
            src_ref=(part if s == BITS - 1 else out_ref).at[rows],
            dst_ref=out_ref.at[rows],
            send_sem=ag_ss.at[s, n],
            recv_sem=ag_rs.at[s, n],
            device_id={"head": partner},
            device_id_type=MESH,
        )

    def own_copy(n):
        keep, give, size, partner = ranges(BITS - 1, n)
        rows = pl.ds(keep, size)
        return pltpu.make_async_copy(part.at[rows], out_ref.at[rows], own_sem.at[n])

    def query_part(n):
        o, w = bounds[n]
        e = min(o + w, FEAT)
        acc = dot_nt(wq_v[0, o:e, :], dq_v[0])
        for c in range(1, NC):
            acc = acc + dot_nt(wq_v[c, o:e, :], dq_v[c])
        return acc

    early = [query_part(n) for n in range(AHEAD)]

    @pl.when(me < D - 1)
    def _():
        halo.wait_recv()

    kvg_b[0 : R - WINDOW] = kvg_f[0 : R - WINDOW].astype(BF16)
    kvg_b[R - WINDOW :] = (kvg_f[R - WINDOW :] + halo_recv[...].astype(F32)).astype(BF16)
    for n, (o, w) in enumerate(bounds):
        e = min(o + w, FEAT)
        acc = early[n] if n < AHEAD else query_part(n)
        acc = acc + dot_nt(wkv_v[o:e, :], kvg_b[...])
        part[o:e, :] = acc.astype(BF16)
        if o + w > e:
            part[e : o + w, :] = jnp.zeros((o + w - e, R), BF16)
        rs_copy(0, n).start()

    for s in range(BITS):
        for n in range(len(bounds)):
            rs_copy(s, n).wait_recv()
            keep, give, size, partner = ranges(s, n)
            added = part[pl.ds(keep, size), :].astype(F32) + rs_recv[landing(s, n), :].astype(F32)
            part[pl.ds(keep, size), :] = added.astype(BF16)
            if s < BITS - 1:
                rs_copy(s + 1, n).start()
            else:
                ag_copy(s, n, True).start()
                own_copy(n).start()

    for s in reversed(range(BITS)):
        for n in range(len(bounds)):
            ag_copy(s, n, False).wait_recv()
            if s == BITS - 1:
                own_copy(n).wait()
            if s > 0:
                ag_copy(s - 1, n, True).start()

    each_peer(lambda p: note_copy(p, me).wait_send())
    each_peer(lambda p: wait_send(kv_copies(p, me)))
    for c in range(NC):
        each_peer(lambda p: wait_send(q_copies(c, p, me)))

    @pl.when(me < D - 1)
    def _():
        edge.wait_send()

    @pl.when(me > 0)
    def _():
        halo.wait_send()

    for s in range(BITS):
        for n in range(len(bounds)):
            rs_copy(s, n).wait_send()
            ag_copy(s, n, True).wait_send()
    loss_store.wait()


def local(hidden, dest_pos, chosen_len, token_logp, head_grad, q_weight, key_value_weight, sinks):
    D, N = lax.axis_size("seq"), lax.axis_size("head")
    R, FEAT = hidden.shape
    HD = key_value_weight.shape[2] // 2
    KH = key_value_weight.shape[1]
    KC = KH * 2 * HD
    QC = q_weight.shape[1]
    PC = chosen_len.shape[0]
    S = -(-(R // D + 1) // 16) * 16
    NC = QC // CHUNK
    BITS = log2(N)
    SLOTS = -(-(D * S) // LANES) * LANES
    bounds = chunk_bounds(FEAT, N)
    NB = len(bounds)
    wide = bounds[-1][0] + bounds[-1][1]
    cfg = (D, N, R, S, QC, KC, FEAT, HD, PC)
    hbm = pl.BlockSpec(memory_space=pltpu.HBM)
    anywhere = pl.BlockSpec(memory_space=pl.ANY)
    dma = pltpu.SemaphoreType.DMA
    grad, loss = pl.pallas_call(
        functools.partial(kernel, cfg),
        out_shape=(
            pltpu.VMEM((wide, R), BF16),
            jax.ShapeDtypeStruct((PC,), F32),
        ),
        in_specs=[hbm] * 8,
        out_specs=(anywhere, hbm),
        scratch_shapes=[
            pltpu.SMEM((PC,), jnp.int32),
            pltpu.SMEM(sinks.shape, F32),
            pltpu.SMEM((PC,), F32),
            pltpu.VMEM((1, R), jnp.int32),
            pltpu.VMEM((1, R), F32),
            pltpu.VMEM((FEAT, R), BF16),
            pltpu.VMEM((R, QC), BF16),
            pltpu.VMEM((NC, FEAT, CHUNK), BF16),
            pltpu.VMEM((FEAT * KH, 2 * HD), BF16),
            pltpu.VMEM((FEAT // 10 * KH, 2 * HD), F32),
            pltpu.VMEM((FEAT, KC), BF16),
            pltpu.VMEM((D * S, FEAT), BF16),
            pltpu.VMEM((D, S, KC), BF16),
            pltpu.VMEM((D, S, KC), BF16),
            pltpu.VMEM((NC, D, S, CHUNK), BF16),
            pltpu.VMEM((NC, D, S, CHUNK), BF16),
            pltpu.VMEM((D, 1, SLOTS + LANES), F32),
            pltpu.VMEM((D, 1, SLOTS + LANES), F32),
            pltpu.VMEM((D, 1, KC), F32),
            pltpu.VMEM((D, 1, KC), F32),
            pltpu.VMEM((NC, D, 1, CHUNK), F32),
            pltpu.VMEM((NC, D, 1, CHUNK), F32),
            pltpu.VMEM((R, D * S), BF16),
            pltpu.VMEM((R + WINDOW, KC), BF16),
            pltpu.VMEM((KH, R + WINDOW, CHUNK), BF16),
            pltpu.VMEM((KH, R + WINDOW, CHUNK), BF16),
            pltpu.VMEM((R // WINDOW, 2 * WINDOW, WINDOW), F32),
            pltpu.VMEM((R, LANES), F32),
            pltpu.VMEM((KH, R + WINDOW, CHUNK), F32),
            pltpu.VMEM((KH, R + WINDOW, CHUNK), F32),
            pltpu.VMEM((NC, R, CHUNK), BF16),
            pltpu.VMEM((R, KC), BF16),
            pltpu.VMEM((R, KC), F32),
            pltpu.VMEM((WINDOW, KC), BF16),
            pltpu.VMEM((WINDOW, KC), BF16),
            pltpu.VMEM((wide, R), BF16),
            pltpu.VMEM((wide, R), BF16),
            dma((5 + NC,)),
            dma((D,)),
            dma((D,)),
            dma((NC, D)),
            dma((NC, D)),
            dma((D,)),
            dma((D,)),
            dma,
            dma,
            dma,
            dma,
            dma((BITS, NB)),
            dma((BITS, NB)),
            dma((BITS, NB)),
            dma((BITS, NB)),
            dma((NB,)),
            dma((3,)),
            dma((D,)),
            dma((D,)),
            dma((NC, D)),
            dma((NC, D)),
        ],
        compiler_params=pltpu.CompilerParams(
            collective_id=0, has_side_effects=True, vmem_limit_bytes=60 * 1024 * 1024
        ),
        name="preference_gradient",
    )(
        chosen_len,
        sinks,
        dest_pos.reshape(1, R),
        token_logp.reshape(1, R),
        hidden.T,
        head_grad,
        q_weight,
        key_value_weight.reshape(FEAT * KH, 2 * HD),
    )
    return grad[:FEAT].T, loss


def solution(mesh):
    placed = (
        P(("batch", "seq"), None),
        P(("batch", "seq")),
        P("batch"),
        P(("batch", "seq")),
        P(("batch", "seq"), "head"),
        P(None, "head"),
        P(None, "head", None),
        P("head"),
    )
    return jax.shard_map(
        local,
        mesh=mesh,
        in_specs=placed,
        out_specs=(P(("batch", "seq"), None), P("batch")),
        check_vma=False,
    )
```

```python
import functools

import jax
import jax.numpy as jnp
from jax import lax
from jax.experimental import pallas as pl
from jax.experimental.pallas import tpu as pltpu
from jax.sharding import PartitionSpec as P

WINDOW = 128
PAIR_POSITIONS = 512
BETA = 2.0
GAMMA = 1.0
LOSS_SCALE = 256.0
NEG_FILL = -1e30
LANES = 128
CHUNK = 256
OUT_CHUNKS = 6
AHEAD = 3
F32 = jnp.float32
BF16 = jnp.bfloat16
MESH = pl.DeviceIdType.MESH


def dot_nn(a, b):
    return lax.dot_general(a, b, (((1,), (0,)), ((), ())), preferred_element_type=F32)


def dot_nt(a, b):
    return lax.dot_general(a, b, (((1,), (1,)), ((), ())), preferred_element_type=F32)


def dot_tn(a, b):
    return lax.dot_general(a, b, (((0,), (0,)), ((), ())), preferred_element_type=F32)


def iota(shape, dim):
    return lax.broadcasted_iota(jnp.int32, shape, dim)


def log2(n):
    assert n & (n - 1) == 0
    return n.bit_length() - 1


def chunk_bounds(feat, n):
    unit = 16 * n
    units = -(-feat // unit)
    count = min(OUT_CHUNKS, units)
    sizes = [unit * ((units + k) // count) for k in range(count)]
    return [(sum(sizes[:k]), sizes[k]) for k in range(count)]


def kernel(
    cfg,
    len_hbm,
    sink_hbm,
    dest_hbm,
    logp_hbm,
    hidden_hbm,
    grad_hbm,
    wq_hbm,
    wkv_hbm,
    out_ref,
    loss_hbm,
    len_ref,
    sink_ref,
    loss_ref,
    dest_v,
    logp_v,
    hidden_v,
    grad_v,
    wq_v,
    wkv_raw,
    wkv_f,
    wkv_v,
    packed_v,
    send_kv,
    recv_kv,
    send_q,
    recv_q,
    note_send,
    note_recv,
    xkv_send,
    xkv_recv,
    xq_send,
    xq_recv,
    place_v,
    kvx,
    k4,
    v4,
    bias_v,
    coef_v,
    dk4,
    dv4,
    dq_v,
    kvg_b,
    kvg_f,
    halo_send,
    halo_recv,
    part,
    rs_recv,
    load_sem,
    kv_ss,
    kv_rs,
    q_ss,
    q_rs,
    note_ss,
    note_rs,
    edge_ss,
    edge_rs,
    halo_ss,
    halo_rs,
    rs_ss,
    rs_rs,
    ag_ss,
    ag_rs,
    own_sem,
    small_sem,
    xkv_ss,
    xkv_rs,
    xq_ss,
    xq_rs,
):
    D, N, R, S, QC, KC, FEAT, HD, PC = cfg
    TRIM = R // D % 16 == 0
    SENT = R // D if TRIM else -(-(R // D + 1) // 8) * 8
    NC = QC // CHUNK
    KH = KC // (2 * HD)
    HPC = CHUNK // HD
    CPK = NC // KH
    BITS = log2(N)
    SLOTS = -(-(D * S) // LANES) * LANES
    scale = HD ** (-0.5)
    me = lax.axis_index("seq")
    hd = lax.axis_index("head")
    bounds = chunk_bounds(FEAT, N)

    loads = [
        pltpu.make_async_copy(dest_hbm, dest_v, load_sem.at[0]),
        pltpu.make_async_copy(hidden_hbm, hidden_v, load_sem.at[1]),
    ]

    def q_load(c):
        columns = pl.ds(pl.multiple_of(c * CHUNK, CHUNK), CHUNK)
        return pltpu.make_async_copy(wq_hbm.at[:, columns], wq_v.at[c], load_sem.at[5 + c])

    logp_load = pltpu.make_async_copy(logp_hbm, logp_v, load_sem.at[2])
    wkv_load = pltpu.make_async_copy(wkv_hbm, wkv_raw, load_sem.at[3])
    grad_load = pltpu.make_async_copy(grad_hbm, grad_v, load_sem.at[4])
    len_load = pltpu.make_async_copy(len_hbm, len_ref, small_sem.at[0])
    sink_load = pltpu.make_async_copy(sink_hbm, sink_ref, small_sem.at[1])
    loss_store = pltpu.make_async_copy(loss_ref, loss_hbm, small_sem.at[2])
    for load in loads:
        load.start(priority=1)
    q_load(0).start(priority=1)
    len_load.start()
    sink_load.start()

    halo_recv[...] = jnp.zeros_like(halo_recv)
    kvx[0:WINDOW] = jnp.zeros((WINDOW, KC), BF16)
    recv_kv[:, S - 16 :, :] = jnp.zeros((D, 16, KC), BF16)
    recv_q[:, :, S - 16 :, :] = jnp.zeros((NC, D, 16, CHUNK), BF16)

    def peer_of(j):
        return lax.rem(me + j, D)

    def bit_of(b):
        return lax.rem(hd // (1 << b), 2)

    def partner_of(b):
        return hd + (1 - 2 * bit_of(b)) * (1 << b)

    barrier = pltpu.get_barrier_semaphore()

    def greet(j, _):
        pl.semaphore_signal(
            barrier, inc=1, device_id={"seq": peer_of(j)}, device_id_type=MESH
        )
        return 0

    lax.fori_loop(1, D, greet, 0)
    for b in range(BITS):
        pl.semaphore_signal(
            barrier, inc=1, device_id={"head": partner_of(b)}, device_id_type=MESH
        )

    loads[0].wait()
    dest = dest_v[...]
    dev = lax.shift_right_arithmetic(dest, jnp.full_like(dest, log2(R)))
    DP = max(16, D)
    hot = jnp.where(dev == iota((DP, R), 0), 1.0, 0.0)
    upper = jnp.where(iota((R, R), 0) < iota((R, R), 1), 1.0, 0.0).astype(BF16)
    before = dot_nn(hot.astype(BF16), upper)
    within = jnp.sum(hot * before, axis=0, keepdims=True).astype(jnp.int32)
    pack = jnp.where(dev * S + within == iota((D * S, R), 0), 1.0, 0.0).astype(BF16)

    loads[1].wait()
    logp_load.start()
    wkv_load.start()
    for o in range(0, FEAT, 4 * LANES):
        w = min(4 * LANES, FEAT - o)
        packed_v[:, o : o + w] = dot_nt(pack, hidden_v[o : o + w, :]).astype(BF16)

    def note_copy(peer, slot):
        return pltpu.make_async_remote_copy(
            src_ref=note_send.at[peer],
            dst_ref=note_recv.at[slot],
            send_sem=note_ss.at[peer],
            recv_sem=note_rs.at[slot],
            device_id={"seq": peer},
            device_id_type=MESH,
        )

    def kv_copy(peer, slot):
        return pltpu.make_async_remote_copy(
            src_ref=send_kv.at[peer, pl.ds(0, SENT)],
            dst_ref=recv_kv.at[slot, pl.ds(0, SENT)],
            send_sem=kv_ss.at[peer],
            recv_sem=kv_rs.at[slot],
            device_id={"seq": peer},
            device_id_type=MESH,
        )

    def q_copy(c, peer, slot):
        return pltpu.make_async_remote_copy(
            src_ref=send_q.at[c, peer, pl.ds(0, SENT)],
            dst_ref=recv_q.at[c, slot, pl.ds(0, SENT)],
            send_sem=q_ss.at[c, peer],
            recv_sem=q_rs.at[c, slot],
            device_id={"seq": peer},
            device_id_type=MESH,
        )

    def xkv_copy(peer, slot):
        return pltpu.make_async_remote_copy(
            src_ref=xkv_send.at[peer],
            dst_ref=xkv_recv.at[slot],
            send_sem=xkv_ss.at[peer],
            recv_sem=xkv_rs.at[slot],
            device_id={"seq": peer},
            device_id_type=MESH,
        )

    def xq_copy(c, peer, slot):
        return pltpu.make_async_remote_copy(
            src_ref=xq_send.at[c, peer],
            dst_ref=xq_recv.at[c, slot],
            send_sem=xq_ss.at[c, peer],
            recv_sem=xq_rs.at[c, slot],
            device_id={"seq": peer},
            device_id_type=MESH,
        )

    def kv_copies(peer, slot):
        return [kv_copy(peer, slot)] + ([xkv_copy(peer, slot)] if TRIM else [])

    def q_copies(c, peer, slot):
        return [q_copy(c, peer, slot)] + ([xq_copy(c, peer, slot)] if TRIM else [])

    def start(copies):
        for copy in copies:
            copy.start()

    def wait_recv(copies):
        for copy in copies:
            copy.wait_recv()

    def wait_send(copies):
        for copy in copies:
            copy.wait_send()

    def put_last(row, block):
        first_row = iota((16, row.shape[-1]), 0) == 0
        block[...] = jnp.where(first_row, row, 0.0).astype(BF16)

    def each_peer(fn):
        def step(j, _):
            fn(peer_of(j))
            return 0

        lax.fori_loop(1, D, step, 0)

    def fill_q(c):
        rows = dot_nn(packed_v[...], wq_v[c]).astype(BF16)
        send_q[c] = rows.reshape(D, S, CHUNK)
        if TRIM:
            for p in range(D):
                xq_send[c, p] = rows[p * S + SENT : p * S + SENT + 1].astype(F32)

    def keep_q(c):
        recv_q[c, me] = send_q[c, me]
        if TRIM:
            xq_recv[c, me] = xq_send[c, me]

    def project(c, _):
        q_load(c).wait()
        fill_q(c)
        keep_q(c)

        @pl.when(c == 1)
        def _():
            each_peer(lambda p: start(q_copies(c, p, me)))

        return 0

    q_load(0).wait()
    for c in range(1, NC):
        q_load(c).start()
    grad_load.start()
    fill_q(0)
    pl.semaphore_wait(barrier, D - 1 + BITS)
    each_peer(lambda p: start(q_copies(0, p, me)))
    keep_q(0)

    place = hot * (dest - dev * R + 1).astype(F32)
    mine = jnp.where(me * S + within == iota((SLOTS, R), 0), 1.0, 0.0)
    places = dot_nt(place.astype(BF16), mine.astype(BF16))
    len_load.wait()
    rotation = (WINDOW // 2 - D // 2 * R) % PAIR_POSITIONS
    total = PC * PAIR_POSITIONS
    first = lax.rem(me * R - WINDOW + rotation + total, total)
    pair_a = first // PAIR_POSITIONS
    pair_b = lax.rem(pair_a + 1, PC)
    len_a = len_ref[pair_a]
    len_b = len_ref[pair_b]

    def segment_of(position):
        u = position + rotation
        u = jnp.where(u >= total, u - total, u)
        pair = lax.shift_right_arithmetic(u, jnp.full_like(u, log2(PAIR_POSITIONS)))
        within = u - pair * PAIR_POSITIONS
        limit = jnp.where(pair == pair_a, len_a, len_b)
        return 2 * pair + jnp.where(within >= limit, 1, 0)

    logp_load.wait()
    row_seg = segment_of(me * R + iota((1, R), 1))
    spread = jnp.where(row_seg == iota((LANES, R), 0), logp_v[...], 0.0)
    local_tot = jnp.sum(spread.T, axis=0, keepdims=True)
    for p in range(D):
        note_send[p, :, 0:SLOTS] = places[p : p + 1, :]
        note_send[p, :, SLOTS:] = local_tot
    each_peer(lambda p: note_copy(p, me).start())
    note_recv[me] = note_send[me]

    wkv_load.wait()
    UNI = FEAT // 10

    def untangle(b, _):
        rows = pl.multiple_of(b * UNI, 16)
        wkv_f[...] = wkv_raw[pl.ds(pl.multiple_of(b * UNI * KH, 16), UNI * KH), :].astype(F32)
        for h in range(KH):
            wkv_v[pl.ds(rows, UNI), h * 2 * HD : (h + 1) * 2 * HD] = wkv_f[
                pl.ds(h, UNI, stride=KH), :
            ].astype(BF16)
        return 0

    lax.fori_loop(0, FEAT // UNI, untangle, 0)
    kv_rows = dot_nn(packed_v[...], wkv_v[...]).astype(BF16)
    send_kv[...] = kv_rows.reshape(D, S, KC)
    if TRIM:
        for p in range(D):
            xkv_send[p] = kv_rows[p * S + SENT : p * S + SENT + 1].astype(F32)
    each_peer(lambda p: start(kv_copies(p, me)))
    recv_kv[me] = send_kv[me]
    if TRIM:
        xkv_recv[me] = xkv_send[me]

    lax.fori_loop(1, NC, project, 0)

    for r in range(R // WINDOW):
        base = me * R + r * WINDOW
        key_pos = base - WINDOW + iota((2 * WINDOW, 1), 0)
        query_pos = base + iota((1, WINDOW), 1)
        offset = query_pos - key_pos
        key_seg = segment_of(key_pos)
        query_seg = segment_of(query_pos)
        allowed = (
            (key_pos >= 0) & (offset >= 0) & (offset < WINDOW) & (key_seg == query_seg)
        )
        bias_v[r] = jnp.where(allowed, 0.0, NEG_FILL)

    each_peer(lambda p: note_copy(p, p).wait_recv())
    notes = jnp.sum(note_recv[...], axis=0)
    place_v[...] = jnp.where(
        iota((R, SLOTS), 0) + 1 == notes[:, 0:SLOTS].astype(jnp.int32), 1.0, 0.0
    ).astype(BF16)[:, 0 : D * S]
    seg_tot = notes[:, SLOTS:]
    lane = iota((1, LANES), 1)
    seg_len = jnp.ones((1, LANES), jnp.int32)
    for p in range(PC):
        seg_len = jnp.where(lane == 2 * p, len_ref[p], seg_len)
        seg_len = jnp.where(lane == 2 * p + 1, PAIR_POSITIONS - len_ref[p], seg_len)
    seg_len = seg_len.astype(F32)
    mean = seg_tot / seg_len
    margin = BETA * (mean - pltpu.roll(mean, LANES - 1, 1)) - GAMMA
    neg = -margin
    tail = jnp.exp(-jnp.abs(neg))
    loss = jnp.maximum(neg, 0.0) + jnp.log1p(tail)
    for p in range(PC):
        loss_ref[p] = jnp.sum(jnp.where(lane == 2 * p, loss, 0.0))
    loss_store.start()
    weight = jnp.where(neg >= 0, 1.0 / (1.0 + tail), tail / (1.0 + tail)) * (BETA * LOSS_SCALE)
    even = (lane & 1) == 0
    coef = jnp.where(even, -weight, pltpu.roll(weight, 1, 1)) / seg_len
    col_seg = segment_of(me * R + iota((R, 1), 0))
    coef_v[...] = jnp.broadcast_to(
        jnp.sum(jnp.where(col_seg == iota((R, LANES), 1), coef, 0.0), axis=1, keepdims=True),
        (R, LANES),
    )

    dk4[...] = jnp.zeros_like(dk4)
    dv4[...] = jnp.zeros_like(dv4)

    each_peer(lambda p: wait_recv(kv_copies(p, p)))
    if NC > 2:
        each_peer(lambda p: start(q_copies(2, p, me)))
    if TRIM:
        for p in range(D):
            put_last(xkv_recv[p], recv_kv.at[p, SENT : SENT + 16])
    kvx[WINDOW:] = dot_nn(place_v[...], recv_kv[...].reshape(D * S, KC)).astype(BF16)

    edge = pltpu.make_async_remote_copy(
        src_ref=kvx.at[pl.ds(R, WINDOW)],
        dst_ref=kvx.at[pl.ds(0, WINDOW)],
        send_sem=edge_ss,
        recv_sem=edge_rs,
        device_id={"seq": lax.rem(me + 1, D)},
        device_id_type=MESH,
    )

    @pl.when(me < D - 1)
    def _():
        edge.start()

    grad_load.wait()

    @pl.when(me > 0)
    def _():
        edge.wait_recv()

    low = iota((R + WINDOW, LANES), 1) < HD
    for h in range(KH):
        kv = kvx[:, h * 2 * HD : (h + 1) * 2 * HD].astype(F32)
        turned = pltpu.roll(kv, HD, 1)
        kk = jnp.where(low, kv, turned).astype(BF16)
        vv = jnp.where(low, turned, kv).astype(BF16)
        for g in range(CHUNK // LANES):
            k4[h, :, g * LANES : (g + 1) * LANES] = kk
            v4[h, :, g * LANES : (g + 1) * LANES] = vv

    head_of = lax.shift_right_arithmetic(
        iota((WINDOW, CHUNK), 1), jnp.full((WINDOW, CHUNK), log2(HD), jnp.int32)
    )

    head_mask = [jnp.where(head_of == g, 1.0, 0.0).astype(BF16) for g in range(HPC)]

    def spread_heads(x):
        return jnp.concatenate(
            [x * head_mask[g] for g in range(HPC)], axis=0
        )

    halo = pltpu.make_async_remote_copy(
        src_ref=halo_send,
        dst_ref=halo_recv,
        send_sem=halo_ss,
        recv_sem=halo_rs,
        device_id={"seq": lax.rem(me + D - 1, D)},
        device_id_type=MESH,
    )

    def fold(h, rows):
        folded = []
        for acc in (dk4, dv4):
            y = acc[h, rows, 0:LANES]
            for g in range(1, CHUNK // LANES):
                y = y + acc[h, rows, g * LANES : (g + 1) * LANES]
            folded.append(y + pltpu.roll(y, HD, 1))
        return jnp.where(low[rows], folded[0], folded[1])

    def attend(c, _):
        h = c // CPK
        each_peer(lambda p: wait_recv(q_copies(c, p, p)))

        @pl.when(c + 3 < NC)
        def _():
            each_peer(lambda p: start(q_copies(c + 3, p, me)))

        if TRIM:
            for p in range(D):
                put_last(xq_recv[c, p], recv_q.at[c, p, SENT : SENT + 16])
        q_all = dot_nn(place_v[...], recv_q[c].reshape(D * S, CHUNK))
        g_all = grad_v[:, pl.ds(c * CHUNK if isinstance(c, int) else pl.multiple_of(c * CHUNK, CHUNK), CHUNK)].astype(F32)
        factor = coef_v[...]
        g_b = (g_all * jnp.concatenate([factor] * (CHUNK // LANES), axis=1)).astype(BF16)
        q_b = (q_all * scale).astype(BF16)
        sink = jnp.concatenate(
            [jnp.full((1, WINDOW), sink_ref[c * HPC + g], F32) for g in range(HPC)], axis=1
        )
        for r in range(R // WINDOW):
            rows = slice(r * WINDOW, (r + 1) * WINDOW)
            keys = slice(r * WINDOW, (r + 2) * WINDOW)
            qz = spread_heads(q_b[rows])
            gz = spread_heads(g_b[rows])
            kr = k4[h, keys, :]
            vr = v4[h, keys, :]
            bias = bias_v[r]
            masked = dot_nt(kr, qz) + jnp.concatenate([bias] * HPC, axis=1)
            top = jnp.maximum(jnp.max(masked, axis=0, keepdims=True), sink)
            expo = jnp.exp(masked - top)
            denom = jnp.exp(sink - top) + jnp.sum(expo, axis=0, keepdims=True)
            probs = expo * (1.0 / denom)
            probs_b = probs.astype(BF16)
            prob_grad = dot_nt(vr, gz)
            row_dot = jnp.sum(probs_b.astype(F32) * prob_grad, axis=0, keepdims=True)
            score_grad = (probs * (prob_grad - row_dot)).astype(BF16)
            dk4[h, keys, :] += dot_nn(score_grad, qz)
            dv4[h, keys, :] += dot_nn(probs_b, gz)
            if r == 0 and isinstance(c, int):
                for k in range(KH):
                    halo_send[:, k * 2 * HD : (k + 1) * 2 * HD] = fold(
                        k, slice(0, WINDOW)
                    ).astype(BF16)

                @pl.when(me > 0)
                def _():
                    halo.start()

            wide = dot_tn(score_grad, kr)
            dq = jnp.where(head_of == 0, wide[0:WINDOW], 0.0)
            for g in range(1, HPC):
                dq = jnp.where(head_of == g, wide[g * WINDOW : (g + 1) * WINDOW], dq)
            dq_v[c, rows, :] = (dq * scale).astype(BF16)
        return 0

    sink_load.wait()
    lax.fori_loop(0, NC - 1, attend, 0)
    attend(NC - 1, 0)

    for h in range(KH):
        cols = slice(h * 2 * HD, (h + 1) * 2 * HD)
        kvg_f[:, cols] = fold(h, slice(WINDOW, WINDOW + R))

    def ranges(s, n):
        off, size = bounds[n]
        order = list(range(BITS)) if n % 2 == 0 else list(reversed(range(BITS)))
        for t in range(s + 1):
            size //= 2
            bit = bit_of(order[t])
            keep = off + bit * size
            give = off + (1 - bit) * size
            off = keep
        return pl.multiple_of(keep, 16), pl.multiple_of(give, 16), size, partner_of(order[s])

    def landing(s, n):
        o, w = bounds[n]
        size = w >> (s + 1)
        return pl.ds(o + w - 2 * size, size)

    def rs_copy(s, n):
        keep, give, size, partner = ranges(s, n)
        return pltpu.make_async_remote_copy(
            src_ref=part.at[pl.ds(give, size)],
            dst_ref=rs_recv.at[landing(s, n)],
            send_sem=rs_ss.at[s, n],
            recv_sem=rs_rs.at[s, n],
            device_id={"head": partner},
            device_id_type=MESH,
        )

    def ag_copy(s, n, mine):
        keep, give, size, partner = ranges(s, n)
        rows = pl.ds(keep if mine else give, size)
        return pltpu.make_async_remote_copy(
            src_ref=(part if s == BITS - 1 else out_ref).at[rows],
            dst_ref=out_ref.at[rows],
            send_sem=ag_ss.at[s, n],
            recv_sem=ag_rs.at[s, n],
            device_id={"head": partner},
            device_id_type=MESH,
        )

    def own_copy(n):
        keep, give, size, partner = ranges(BITS - 1, n)
        rows = pl.ds(keep, size)
        return pltpu.make_async_copy(part.at[rows], out_ref.at[rows], own_sem.at[n])

    def query_part(n):
        o, w = bounds[n]
        e = min(o + w, FEAT)
        acc = dot_nt(wq_v[0, o:e, :], dq_v[0])
        for c in range(1, NC):
            acc = acc + dot_nt(wq_v[c, o:e, :], dq_v[c])
        return acc

    early = [query_part(n) for n in range(AHEAD)]

    @pl.when(me < D - 1)
    def _():
        halo.wait_recv()

    kvg_b[0 : R - WINDOW] = kvg_f[0 : R - WINDOW].astype(BF16)
    kvg_b[R - WINDOW :] = (kvg_f[R - WINDOW :] + halo_recv[...].astype(F32)).astype(BF16)
    for n, (o, w) in enumerate(bounds):
        e = min(o + w, FEAT)
        acc = early[n] if n < AHEAD else query_part(n)
        acc = acc + dot_nt(wkv_v[o:e, :], kvg_b[...])
        part[o:e, :] = acc.astype(BF16)
        if o + w > e:
            part[e : o + w, :] = jnp.zeros((o + w - e, R), BF16)
        rs_copy(0, n).start()

    for s in range(BITS):
        for n in range(len(bounds)):
            rs_copy(s, n).wait_recv()
            keep, give, size, partner = ranges(s, n)
            added = part[pl.ds(keep, size), :].astype(F32) + rs_recv[landing(s, n), :].astype(F32)
            part[pl.ds(keep, size), :] = added.astype(BF16)
            if s < BITS - 1:
                rs_copy(s + 1, n).start()
            else:
                ag_copy(s, n, True).start()
                own_copy(n).start()

    for s in reversed(range(BITS)):
        for n in range(len(bounds)):
            ag_copy(s, n, False).wait_recv()
            if s == BITS - 1:
                own_copy(n).wait()
            if s > 0:
                ag_copy(s - 1, n, True).start()

    each_peer(lambda p: note_copy(p, me).wait_send())
    each_peer(lambda p: wait_send(kv_copies(p, me)))
    for c in range(NC):
        each_peer(lambda p: wait_send(q_copies(c, p, me)))

    @pl.when(me < D - 1)
    def _():
        edge.wait_send()

    @pl.when(me > 0)
    def _():
        halo.wait_send()

    for s in range(BITS):
        for n in range(len(bounds)):
            rs_copy(s, n).wait_send()
            ag_copy(s, n, True).wait_send()
    loss_store.wait()


def local(hidden, dest_pos, chosen_len, token_logp, head_grad, q_weight, key_value_weight, sinks):
    D, N = lax.axis_size("seq"), lax.axis_size("head")
    R, FEAT = hidden.shape
    HD = key_value_weight.shape[2] // 2
    KH = key_value_weight.shape[1]
    KC = KH * 2 * HD
    QC = q_weight.shape[1]
    PC = chosen_len.shape[0]
    S = -(-(R // D + 1) // 16) * 16
    NC = QC // CHUNK
    BITS = log2(N)
    SLOTS = -(-(D * S) // LANES) * LANES
    bounds = chunk_bounds(FEAT, N)
    NB = len(bounds)
    wide = bounds[-1][0] + bounds[-1][1]
    cfg = (D, N, R, S, QC, KC, FEAT, HD, PC)
    hbm = pl.BlockSpec(memory_space=pltpu.HBM)
    anywhere = pl.BlockSpec(memory_space=pl.ANY)
    dma = pltpu.SemaphoreType.DMA
    grad, loss = pl.pallas_call(
        functools.partial(kernel, cfg),
        out_shape=(
            pltpu.VMEM((wide, R), BF16),
            jax.ShapeDtypeStruct((PC,), F32),
        ),
        in_specs=[hbm] * 8,
        out_specs=(anywhere, hbm),
        scratch_shapes=[
            pltpu.SMEM((PC,), jnp.int32),
            pltpu.SMEM(sinks.shape, F32),
            pltpu.SMEM((PC,), F32),
            pltpu.VMEM((1, R), jnp.int32),
            pltpu.VMEM((1, R), F32),
            pltpu.VMEM((FEAT, R), BF16),
            pltpu.VMEM((R, QC), BF16),
            pltpu.VMEM((NC, FEAT, CHUNK), BF16),
            pltpu.VMEM((FEAT * KH, 2 * HD), BF16),
            pltpu.VMEM((FEAT // 10 * KH, 2 * HD), F32),
            pltpu.VMEM((FEAT, KC), BF16),
            pltpu.VMEM((D * S, FEAT), BF16),
            pltpu.VMEM((D, S, KC), BF16),
            pltpu.VMEM((D, S, KC), BF16),
            pltpu.VMEM((NC, D, S, CHUNK), BF16),
            pltpu.VMEM((NC, D, S, CHUNK), BF16),
            pltpu.VMEM((D, 1, SLOTS + LANES), F32),
            pltpu.VMEM((D, 1, SLOTS + LANES), F32),
            pltpu.VMEM((D, 1, KC), F32),
            pltpu.VMEM((D, 1, KC), F32),
            pltpu.VMEM((NC, D, 1, CHUNK), F32),
            pltpu.VMEM((NC, D, 1, CHUNK), F32),
            pltpu.VMEM((R, D * S), BF16),
            pltpu.VMEM((R + WINDOW, KC), BF16),
            pltpu.VMEM((KH, R + WINDOW, CHUNK), BF16),
            pltpu.VMEM((KH, R + WINDOW, CHUNK), BF16),
            pltpu.VMEM((R // WINDOW, 2 * WINDOW, WINDOW), F32),
            pltpu.VMEM((R, LANES), F32),
            pltpu.VMEM((KH, R + WINDOW, CHUNK), F32),
            pltpu.VMEM((KH, R + WINDOW, CHUNK), F32),
            pltpu.VMEM((NC, R, CHUNK), BF16),
            pltpu.VMEM((R, KC), BF16),
            pltpu.VMEM((R, KC), F32),
            pltpu.VMEM((WINDOW, KC), BF16),
            pltpu.VMEM((WINDOW, KC), BF16),
            pltpu.VMEM((wide, R), BF16),
            pltpu.VMEM((wide, R), BF16),
            dma((5 + NC,)),
            dma((D,)),
            dma((D,)),
            dma((NC, D)),
            dma((NC, D)),
            dma((D,)),
            dma((D,)),
            dma,
            dma,
            dma,
            dma,
            dma((BITS, NB)),
            dma((BITS, NB)),
            dma((BITS, NB)),
            dma((BITS, NB)),
            dma((NB,)),
            dma((3,)),
            dma((D,)),
            dma((D,)),
            dma((NC, D)),
            dma((NC, D)),
        ],
        compiler_params=pltpu.CompilerParams(
            collective_id=0, has_side_effects=True, vmem_limit_bytes=60 * 1024 * 1024
        ),
        name="preference_gradient",
    )(
        chosen_len,
        sinks,
        dest_pos.reshape(1, R),
        token_logp.reshape(1, R),
        hidden.T,
        head_grad,
        q_weight,
        key_value_weight.reshape(FEAT * KH, 2 * HD),
    )
    return grad[:FEAT].T, loss


def solution(mesh):
    placed = (
        P(("batch", "seq"), None),
        P(("batch", "seq")),
        P("batch"),
        P(("batch", "seq")),
        P(("batch", "seq"), "head"),
        P(None, "head"),
        P(None, "head", None),
        P("head"),
    )
    return jax.shard_map(
        local,
        mesh=mesh,
        in_specs=placed,
        out_specs=(P(("batch", "seq"), None), P("batch")),
        check_vma=False,
    )
```
